256 devices in a mesh: lon: 16 (over y, x), lat: 8 (over z), mem: 2 (over core).
Axes of the slice: x: 4, y: 4, z: 8, core: 2. Of those that a mesh axis runs over, the one named last changes fastest.
Arguments:
- anomalies: bfloat16 [128, 128, 4096], P('mem', 'lat', 'lon'), may hold values from -6 to 6
- state_mean: float32 [128, 4096], P('lat', 'lon'), may hold values from -6 to 6
- delayed_deviation_pair: bfloat16 [2, 128, 128, 4096], P(None, 'mem', 'lat', 'lon'), may hold values from -6 to 6
- lagged_means: float32 [2, 128, 4096], P(None, 'lat', 'lon'), may hold values from -6 to 6
- courant_lon: float32 [128, 4096], P('lat', 'lon'), may hold values from -0.45 to 0.45
- courant_lat: float32 [128, 4096], P('lat', 'lon'), may hold values from -0.45 to 0.45
- ocean: int32 [128, 4096], P('lat', 'lon'), may hold values 0 or 1
- obs_values: float32 [16384, 64], P(('lon', 'lat')), may hold values from -160 to 160
- obs_variance: float32 [16384, 64], P(('lon', 'lat')), may hold values from 2048 to 32768
- obs_cells: int32 [16384, 64], P(('lon', 'lat')), may hold values from 0 to 4095
- obs_tile: int32 [16384, 1], P(('lon', 'lat')), may hold values from 0 to 127; in each aligned block of 128 rows (0 to 127, 128 to 255, ...) at most 2 rows name the same one
- obs_count: int32 [16384], P(('lon', 'lat')), may hold values from 48 to 64
Outputs:
- analysis_anomalies: bfloat16 [3, 128, 128, 4096], P(None, 'mem', 'lat', 'lon')
- analysis_mean: float32 [3, 128, 4096], P(None, 'lat', 'lon')
The draws below stay inside these ranges and needn't reach their ends.
Inputs may be any that keep to these rules, and one draw needn't show every extreme that they name: `obs_tile`: among the 128 blocks of one tile (an aligned run of rows) no tile is named more than 2 times.
All inputs are finite; a program needn't handle non-finite values. Where the reference program divides by a largest or mean magnitude, that divisor is 1e-20 or more. No bound on the sum of `ocean` on one device may be relied on, other than what follows from the above.
Results may differ from the reference program's by a relative error of at most 0.0034.
Values may be sent and summed in bfloat16 or wider, within the bound.
A program may use at most 64 MiB of HBM per device.

```python
import math
import jax
import jax.numpy as jnp
import numpy as np
from jax import lax

SAMPLE_TALLY = 128
CY = 16
CX = 256
SUBSTEPS = 4
NS_ITERS = 8
BLK_DEV = 128
OBS_LEN = 64
TILES = 128
CAP = 2
BLOCKS = 16384
MERIDIAN_SPAN = 128
PARALLEL_SPAN = 4096


def plant(drawn, stream_key, low, largest):
    longest = drawn.shape.index(max(drawn.shape))
    spots = []
    for shift in (0, 1):
        where = [jax.random.randint(jax.random.fold_in(stream_key, axis), (), 0, length) for axis, length in enumerate(drawn.shape)]
        where[longest] = (where[longest] + shift) % drawn.shape[longest]
        spots.append(tuple(where))
    return drawn.at[spots[0]].set(low).at[spots[1]].set(largest)


def shard_levels(rng, dims, shards, low, largest):
    level, own = 1.0, jax.random.fold_in(rng, 6)
    for dim, blocks in shards:
        draws = jnp.exp(jax.random.uniform(jax.random.fold_in(own, dim), (blocks,), jnp.float32, low / len(shards), largest / len(shards)))
        level = level * jnp.repeat(draws, dims[dim] // blocks).reshape([-1 if axis == dim else 1 for axis in range(len(dims))])
    return level


def routed_block(stream_key, own, number, rows, count, top, most, lean):
    order = jax.random.permutation(stream_key, count)
    packed, usual = shares(count, rows * top, most, lean, True), shares(count, rows * top, most, lean, False)
    places = jnp.arange(count)

    def named(tallies, offset_by):
        used = int((tallies > 0).sum())
        fixed = max(1, used // 4)
        moved = fixed + (places - fixed + offset_by * (used - fixed)) % max(1, count - fixed)
        return jnp.zeros((count,), jnp.int32).at[order[jnp.where(places < fixed, places, moved)]].set(jnp.asarray(tallies, jnp.int32))

    tallies = jnp.where(number % 4 == 0, named(packed, number // 4), named(usual, number - number // 4 - 1))
    mixed = jax.random.permutation(jax.random.fold_in(own, 3), count)
    source_of, sink = mixed[0:count // 2 * 2:2], mixed[1:count // 2 * 2:2]
    margin = jnp.minimum(tallies[source_of] - 1, most - tallies[sink]) // 2
    margin = jnp.where((source_of == order[0]) | (sink == order[0]) | (tallies[sink] == 0), 0, jnp.maximum(margin, 0))
    moved = jax.random.randint(jax.random.fold_in(own, 4), (count // 2,), 0, 1 << 20) % (margin + 1)
    tallies = tallies.at[source_of].add(-moved).at[sink].add(moved)
    items = jnp.searchsorted(jnp.cumsum(tallies), jnp.arange(rows * top), side="right").astype(jnp.int32)
    listing = items.reshape(top, rows).T
    listing = listing[jax.random.permutation(jax.random.fold_in(own, 1), rows)]
    offset_by = jax.random.randint(jax.random.fold_in(own, 2), (rows, 1), 0, top)
    return jnp.take_along_axis(listing, (jnp.arange(top)[None, :] + offset_by) % top, axis=1)


def shares(amount, total, reach, lean, full):
    weights = [(1 << 20) // math.isqrt(standing ** lean) + 1 for standing in range(1, amount + 1)]
    largest = reach if full else min(reach, max(-(-total // amount), total * weights[0] // sum(weights)))
    least = 1 if total - largest >= amount - 1 else 0
    counts, surplus = [largest] + [least] * (amount - 1), total - largest - least * (amount - 1)
    while surplus > 0:
        candidates = [i for i in range(1, amount) if counts[i] < largest] or [i for i in range(1, amount) if counts[i] < reach]
        mass, left = sum([weights[i] for i in candidates]), surplus
        for i in candidates:
            extra = min(reach - counts[i], max(1, left * weights[i] // mass), surplus)
            counts[i] = counts[i] + extra
            surplus = surplus - extra
    return np.array(counts)


def gaussian(rng, shape, spread, most, pieces=(), held_as=jnp.bfloat16):
    entries = jax.random.normal(rng, shape, jnp.float32) * spread
    if len(pieces) > 0:
        entries = shard_levels(rng, shape, pieces, -0.22, 0.18) * entries
    return jnp.clip(entries, min=-most, max=most).astype(held_as)


def setup_inputs(seed: int = 0) -> dict:
    arg_keys = jax.random.split(jax.random.key(seed), 13)
    anomalies = gaussian(arg_keys[0], (SAMPLE_TALLY, MERIDIAN_SPAN, PARALLEL_SPAN), 1.0, 6.0, ((0, 2), (1, 8), (2, 16)))
    state_mean = gaussian(arg_keys[1], (MERIDIAN_SPAN, PARALLEL_SPAN), 1.0, 6.0, ((0, 8), (1, 16)), jnp.float32)
    delayed_deviation_pair = gaussian(arg_keys[2], (2, SAMPLE_TALLY, MERIDIAN_SPAN, PARALLEL_SPAN), 1.0, 6.0, ((1, 2), (2, 8), (3, 16)))
    lagged_means = gaussian(arg_keys[3], (2, MERIDIAN_SPAN, PARALLEL_SPAN), 1.0, 6.0, ((1, 8), (2, 16)), jnp.float32)
    courant_lon = jnp.clip(jax.random.uniform(arg_keys[4], (MERIDIAN_SPAN, PARALLEL_SPAN), jnp.float32, -0.45, 0.45) * shard_levels(arg_keys[4], (MERIDIAN_SPAN, PARALLEL_SPAN), ((0, 8), (1, 16)), -0.4, 0.0), -0.45, 0.45)
    courant_lat = jnp.clip(jax.random.uniform(arg_keys[5], (MERIDIAN_SPAN, PARALLEL_SPAN), jnp.float32, -0.45, 0.45) * shard_levels(arg_keys[5], (MERIDIAN_SPAN, PARALLEL_SPAN), ((0, 8), (1, 16)), -0.4, 0.0), -0.45, 0.45)
    ocean = plant((jax.random.randint(arg_keys[6], (MERIDIAN_SPAN, PARALLEL_SPAN), 0, 10) < 7).astype(jnp.int32), jax.random.fold_in(arg_keys[6], 1), 0, 1)
    obs_values = gaussian(arg_keys[7], (BLOCKS, OBS_LEN), 32, 160.0, ((0, 128),), jnp.float32)
    obs_variance = jnp.clip(jnp.exp(math.log(32768.0) - 2.7725887 * jax.random.uniform(arg_keys[8], (BLOCKS, OBS_LEN), jnp.float32) ** shard_levels(arg_keys[8], (BLOCKS, OBS_LEN), ((0, 128),), -0.2, 0.2)), 2048.0, 32768.0)
    obs_cells = plant(jax.random.randint(arg_keys[9], (BLOCKS, OBS_LEN), 0, CY * CX), jax.random.fold_in(arg_keys[9], 1), 0, (CY * CX) - 1).astype(jnp.int32)
    obs_tile_keys = jax.random.split(jax.random.fold_in(arg_keys[10], 1), BLOCKS // BLK_DEV)
    obs_tile_turns = jax.random.permutation(jax.random.fold_in(arg_keys[10], 3), BLOCKS // BLK_DEV)
    obs_tile = jax.vmap(lambda own, number: routed_block(jax.random.fold_in(arg_keys[10], 2), own, number, BLK_DEV, TILES, 1, CAP, 2))(obs_tile_keys, obs_tile_turns).reshape((BLOCKS, 1))
    obs_count = plant(jax.random.randint(arg_keys[11], (BLOCKS,), 3 * OBS_LEN // 4, OBS_LEN + 1), jax.random.fold_in(arg_keys[11], 1), 3 * OBS_LEN // 4, OBS_LEN).astype(jnp.int32)
    return {"anomalies": anomalies, "state_mean": state_mean, "delayed_deviation_pair": delayed_deviation_pair, "lagged_means": lagged_means, "courant_lon": courant_lon, "courant_lat": courant_lat, "ocean": ocean, "obs_values": obs_values, "obs_variance": obs_variance, "obs_cells": obs_cells, "obs_tile": obs_tile, "obs_count": obs_count}


group_rows = 64

def upwind(center, western, eastern, southern, northern, courant_x, courant_y, wet_mask):
    tendency = jnp.maximum(courant_x, 0.0) * (center - western) + jnp.minimum(courant_x, 0.0) * (eastern - center) + jnp.maximum(courant_y, 0.0) * (center - southern) + jnp.minimum(courant_y, 0.0) * (northern - center)
    return center - wet_mask * tendency

def inverse_root(gram, projection):
    members = gram.shape[0]
    identity = jnp.eye(members, dtype=jnp.float32)
    system = (members - 1.0) * identity + 0.5 * (gram + gram.T)
    bound = jnp.max(lax.optimization_barrier(jnp.sum(jnp.abs(system), axis=1)))
    iterate = system / bound
    accum = identity
    for sweep in range(NS_ITERS):
        factor = 1.5 * identity - 0.5 * jnp.dot(accum, iterate, precision=lax.Precision.HIGHEST)
        iterate = jnp.dot(iterate, factor, precision=lax.Precision.HIGHEST)
        accum = jnp.dot(factor, accum, precision=lax.Precision.HIGHEST)
    root = accum / jnp.sqrt(bound)
    weights = jnp.dot(root, jnp.dot(root, projection, precision=lax.Precision.HIGHEST), precision=lax.Precision.HIGHEST)
    transform = jnp.sqrt(members - 1.0) * root
    return (transform.astype(jnp.bfloat16), weights.astype(jnp.bfloat16))

def reference(anomalies, state_mean, delayed_deviation_pair, lagged_means, courant_lon, courant_lat, ocean, obs_values, obs_variance, obs_cells, obs_tile, obs_count):
    wet_mask = ocean.astype(jnp.float32)

    def advect_member(member_field):
        for substep in range(SUBSTEPS):
            padded = jnp.pad(member_field, ((1, 1), (0, 0)))
            member_field = upwind(member_field, jnp.roll(member_field, 1, axis=1), jnp.roll(member_field, -1, axis=1), padded[:-2], padded[2:], courant_lon, courant_lat, wet_mask)
        return member_field
    sample_surfaces = jnp.concatenate([anomalies.astype(jnp.float32), state_mean[None]], 0)
    advanced_sample_vectors = lax.map(advect_member, sample_surfaces)
    predicted_sample_vectors = advanced_sample_vectors[:SAMPLE_TALLY].astype(jnp.bfloat16)
    prior_mean = advanced_sample_vectors[SAMPLE_TALLY]
    raveled_sample_vector = predicted_sample_vectors.reshape(SAMPLE_TALLY, MERIDIAN_SPAN * PARALLEL_SPAN)
    flattened_mean = prior_mean.reshape(-1)
    lat_bands = MERIDIAN_SPAN // CY
    target = obs_tile[:, 0]
    lon_band = target // lat_bands
    lat_band = target % lat_bands
    row_index = lat_band[:, None] * CY + obs_cells // CX
    col_index = lon_band[:, None] * CX + obs_cells % CX
    global_cells = (row_index * PARALLEL_SPAN + col_index).astype(jnp.int32)
    batches = BLOCKS // group_rows

    def gram_step(totals, inputs):
        cells_block, values_block, variance_block, count_block = inputs
        valid = jnp.arange(OBS_LEN, dtype=jnp.int32)[None, :] < count_block[:, None]
        weight = jnp.where(valid, 1.0 / variance_block, 0.0).reshape(-1)
        flat_cells = cells_block.reshape(-1)
        observed = raveled_sample_vector[:, flat_cells]
        weighted = (observed.astype(jnp.float32) * weight).astype(jnp.bfloat16)
        obs_misfit = (values_block.reshape(-1) - flattened_mean[flat_cells]).astype(jnp.bfloat16)
        gram = totals[0] + lax.dot_general(weighted, observed, (((1,), (1,)), ((), ())), preferred_element_type=jnp.float32)
        projection = totals[1] + jnp.dot(weighted, obs_misfit, preferred_element_type=jnp.float32)
        return ((gram, projection), None)
    inputs = (global_cells.reshape(batches, group_rows, OBS_LEN), obs_values.reshape(batches, group_rows, OBS_LEN), obs_variance.reshape(batches, group_rows, OBS_LEN), obs_count.reshape(batches, group_rows))
    start_totals = (jnp.zeros((SAMPLE_TALLY, SAMPLE_TALLY), jnp.float32), jnp.zeros((SAMPLE_TALLY,), jnp.float32))
    (gram, projection), unused = lax.scan(gram_step, start_totals, inputs)
    transform, weights = inverse_root(gram, projection)
    marine_sample_vectors = [predicted_sample_vectors, delayed_deviation_pair[0], delayed_deviation_pair[1]]
    state_means = [prior_mean, lagged_means[0], lagged_means[1]]
    wet_flat = wet_mask.reshape(-1)
    anomaly_outs = []
    mean_outs = []
    for which in range(3):
        source = marine_sample_vectors[which].reshape(SAMPLE_TALLY, MERIDIAN_SPAN * PARALLEL_SPAN)
        moved = jnp.dot(transform.T, source, preferred_element_type=jnp.float32)
        increment = jnp.dot(weights, source, preferred_element_type=jnp.float32)
        source_float = source.astype(jnp.float32)
        blended = (source_float + wet_flat * (moved - source_float)).astype(jnp.bfloat16)
        anomaly_outs.append(blended.reshape(SAMPLE_TALLY, MERIDIAN_SPAN, PARALLEL_SPAN))
        mean_outs.append(state_means[which] + wet_mask * increment.reshape(MERIDIAN_SPAN, PARALLEL_SPAN))
    return (jnp.stack(anomaly_outs), jnp.stack(mean_outs))
```

```python
import math

import jax
import jax.numpy as jnp
from jax import lax
from jax.sharding import Mesh
from jax.sharding import PartitionSpec as P

SUBSTEPS = 4
NS_ITERS = 8
LON = ("lon_0", "lon_1")
LON_LAT = ("lon_0", "lon_1", "lat")


def with_halo(x, sides, width, wrap):
    for axis, dim in sides:
        count, length = (lax.axis_size(axis), x.shape[dim])
        up = [(i, (i + 1) % count) for i in range(count if wrap else count - 1)]
        down = [(j, i) for i, j in up]
        last = lax.slice_in_dim(x, length - width, length, axis=dim)
        leading = lax.slice_in_dim(x, 0, width, axis=dim)
        before = lax.ppermute(last, axis, up)
        after = lax.ppermute(leading, axis, down)
        x = jnp.concatenate([before, x, after], axis=dim)
    return x


def sent_together(arrays, axis, split_dim, concat_dim, along):
    widths = [a.shape[along] for a in arrays]
    both = jnp.concatenate(arrays, axis=along)
    out = lax.all_to_all(both, axis, split_axis=split_dim, concat_axis=concat_dim, tiled=True)
    return tuple(jnp.split(out, [sum(widths[:k]) for k in range(1, len(widths))], axis=along))


def over_axes(x, axes):
    for axis in axes:
        x = lax.psum(x, axis)
    return x


def side_by_side(arrays, axis, dim, along):
    widths = [math.prod(a.shape[along:]) for a in arrays]
    both = jnp.concatenate(
        [a.reshape(*a.shape[:along], w) for a, w in zip(arrays, widths)], axis=along
    )
    out = lax.all_gather(both, axis, axis=dim, tiled=True)
    blocks = jnp.split(out, [sum(widths[:k]) for k in range(1, len(widths))], axis=along)
    return tuple((b.reshape(*out.shape[:along], *a.shape[along:]) for a, b in zip(arrays, blocks)))


def upwind(center, western, eastern, southern, northern, courant_x, courant_y, wet_mask):
    tendency = (
        jnp.maximum(courant_x, 0.0) * (center - western)
        + jnp.minimum(courant_x, 0.0) * (eastern - center)
        + jnp.maximum(courant_y, 0.0) * (center - southern)
        + jnp.minimum(courant_y, 0.0) * (northern - center)
    )
    return center - wet_mask * tendency


def inverse_root(gram, projection):
    members = gram.shape[0]
    identity = jnp.eye(members, dtype=jnp.float32)
    system = (members - 1.0) * identity + 0.5 * (gram + gram.T)
    bound = jnp.max(jnp.sum(jnp.abs(system), axis=1))
    iterate = system / bound
    accum = identity
    for sweep in range(NS_ITERS):
        factor = 1.5 * identity - 0.5 * jnp.dot(accum, iterate, precision=lax.Precision.HIGHEST)
        iterate = jnp.dot(iterate, factor, precision=lax.Precision.HIGHEST)
        accum = jnp.dot(factor, accum, precision=lax.Precision.HIGHEST)
    root = accum / jnp.sqrt(bound)
    weights = jnp.dot(
        root,
        jnp.dot(root, projection, precision=lax.Precision.HIGHEST),
        precision=lax.Precision.HIGHEST,
    )
    transform = jnp.sqrt(members - 1.0) * root
    return (transform.astype(jnp.bfloat16), weights.astype(jnp.bfloat16))


def body(
    anomalies,
    state_mean,
    delayed_deviation_pair,
    lagged_means,
    courant_lon,
    courant_lat,
    ocean,
    obs_values,
    obs_variance,
    obs_cells,
    obs_tile,
    obs_count,
):
    locally_held_samples = anomalies.shape[0]
    wet_mask = ocean.astype(jnp.float32)
    coefficients = jnp.stack([courant_lon, courant_lat, wet_mask])
    sample_surfaces = jnp.concatenate([anomalies.astype(jnp.float32), state_mean[None]], 0)
    stacked = jnp.concatenate([sample_surfaces, coefficients], 0)
    widened = with_halo(stacked, ((LON, 2),), SUBSTEPS, True)
    extended = with_halo(widened.astype(jnp.bfloat16), (("lat", 1),), SUBSTEPS, False).astype(
        widened.dtype
    )
    field_count = sample_surfaces.shape[0]
    sample_surfaces = extended[:field_count]
    beside_all = extended[field_count:]
    for substep in range(SUBSTEPS):
        inner = beside_all[
            :,
            substep + 1 : beside_all.shape[1] - substep - 1,
            substep + 1 : beside_all.shape[2] - substep - 1,
        ]
        sample_surfaces = upwind(
            sample_surfaces[:, 1:-1, 1:-1],
            sample_surfaces[:, 1:-1, :-2],
            sample_surfaces[:, 1:-1, 2:],
            sample_surfaces[:, :-2, 1:-1],
            sample_surfaces[:, 2:, 1:-1],
            inner[0],
            inner[1],
            inner[2],
        )
    predicted_sample_vectors = sample_surfaces[:locally_held_samples].astype(jnp.bfloat16)
    prior_mean = sample_surfaces[locally_held_samples]
    total_cells = prior_mean.shape[0] * prior_mean.shape[1]
    tiles = lax.axis_size(LON_LAT)
    block_total = obs_values.shape[0]
    slot_width = obs_values.shape[1]
    capacity = 2 * block_total // tiles
    target = obs_tile[:, 0]
    block_order = jnp.arange(block_total, dtype=jnp.int32)
    same_target = target[:, None] == target[None, :]
    earlier = block_order[:, None] > block_order[None, :]
    position = jnp.sum((same_target & earlier).astype(jnp.int32), 1)
    destination = target * capacity + position
    placement_table = (
        destination[:, None] == jnp.arange(tiles * capacity, dtype=jnp.int32)[None, :]
    ).astype(jnp.float32)
    valid = jnp.arange(slot_width, dtype=jnp.int32)[None, :] < obs_count[:, None]
    weight = jnp.where(valid, 1.0 / obs_variance, 0.0)
    packed = jnp.concatenate([obs_values, weight, obs_cells.astype(jnp.float32)], 1)
    placed = lax.dot_general(
        placement_table, packed, (((0,), (0,)), ((), ())), precision=lax.Precision.HIGHEST
    ).reshape(tiles, capacity, 3, slot_width)
    arrived_values = sent_together(
        (placed[:, :, 0], placed[:, :, 1], placed[:, :, 2]), LON_LAT, 0, 0, 1
    )
    grid_cells = arrived_values[2].reshape(-1).astype(jnp.int32)
    obs_weight = arrived_values[1].reshape(-1)
    scaled_value = obs_weight * arrived_values[0].reshape(-1)
    rows, columns = (prior_mean.shape[0], prior_mean.shape[1])
    planes = []
    for plane in (obs_weight, scaled_value):
        upper = plane.astype(jnp.bfloat16)
        planes += [upper, (plane - upper.astype(jnp.float32)).astype(jnp.bfloat16)]
    in_row = (grid_cells // columns)[None, :] == jnp.arange(rows, dtype=jnp.int32)[:, None]
    in_column = (grid_cells % columns)[None, :] == jnp.arange(columns, dtype=jnp.int32)[:, None]
    spread = jnp.concatenate(
        [jnp.where(in_row, p[None, :], jnp.zeros((), jnp.bfloat16)) for p in planes], 0
    )
    sums = lax.dot_general(
        spread,
        in_column.astype(jnp.bfloat16),
        (((1,), (1,)), ((), ())),
        preferred_element_type=jnp.float32,
    ).reshape(2, 2, rows, columns)
    cell_weight = sums[0, 0] + sums[0, 1]
    cell_misfit = (sums[1, 0] + sums[1, 1]) - cell_weight * prior_mean
    observed = predicted_sample_vectors.reshape(locally_held_samples, total_cells)
    weighted = (observed.astype(jnp.float32) * cell_weight.reshape(-1)).astype(jnp.bfloat16)
    observed_all = lax.all_gather(observed, "mem", axis=0, tiled=True)
    gram_part = lax.dot_general(
        weighted, observed_all, (((1,), (1,)), ((), ())), preferred_element_type=jnp.float32
    )
    projection_part = lax.dot_general(
        observed,
        cell_misfit.reshape(-1).astype(jnp.bfloat16),
        (((1,), (0,)), ((), ())),
        preferred_element_type=jnp.float32,
    )
    gram_part, projection_part = (
        over_axes(gram_part, LON_LAT),
        over_axes(projection_part, LON_LAT),
    )
    gram, projection = side_by_side((gram_part, projection_part), "mem", 0, 1)
    transform, weights = inverse_root(gram, projection)
    marine_sample_vectors = jnp.concatenate(
        [predicted_sample_vectors[None], delayed_deviation_pair], 0
    )
    flat_states = marine_sample_vectors.reshape(3, locally_held_samples, total_cells)
    first_member = lax.axis_index("mem") * locally_held_samples
    own_columns = lax.dynamic_slice_in_dim(transform, first_member, locally_held_samples, 1)
    segment = lax.all_gather(marine_sample_vectors, "mem", axis=1, tiled=True)
    length = segment.shape[1]
    flat_segment = segment.reshape(3, length, total_cells)
    moved_sum = jnp.einsum(
        "nk,snc->skc", own_columns, flat_segment, preferred_element_type=jnp.float32
    )
    increment_sum = jnp.einsum(
        "n,snc->sc", weights, flat_segment, preferred_element_type=jnp.float32
    )
    wet_flat = wet_mask.reshape(-1)
    states_float = flat_states.astype(jnp.float32)
    blended = (states_float + wet_flat * (moved_sum - states_float)).astype(jnp.bfloat16)
    analysis_anomalies = blended.reshape(marine_sample_vectors.shape)
    state_means = jnp.concatenate([prior_mean[None], lagged_means], 0)
    analysis_mean = state_means + wet_mask * increment_sum.reshape(state_means.shape)
    return (analysis_anomalies, analysis_mean)


def solution(mesh):
    finer = Mesh(
        mesh.devices.reshape(4, 4, mesh.shape["lat"], mesh.shape["mem"]),
        ("lon_0", "lon_1", "lat", "mem"),
    )
    return jax.shard_map(
        body,
        mesh=finer,
        in_specs=(
            P("mem", "lat", LON),
            P("lat", LON),
            P(None, "mem", "lat", LON),
            P(None, "lat", LON),
            P("lat", LON),
            P("lat", LON),
            P("lat", LON),
            P(LON_LAT, None),
            P(LON_LAT, None),
            P(LON_LAT, None),
            P(LON_LAT, None),
            P(LON_LAT),
        ),
        out_specs=(P(None, "mem", "lat", LON), P(None, "lat", LON)),
        check_vma=False,
    )
```

```python
import functools

import jax
import jax.numpy as jnp
from jax import lax
from jax.experimental import pallas as pl
from jax.experimental.pallas import tpu as pltpu
from jax.sharding import PartitionSpec as P

SUBSTEPS = 4
NS_ITERS = 8
BF = jnp.bfloat16
F32 = jnp.float32
MESH_ID = pl.DeviceIdType.MESH
LIMIT = 48 * 1024 * 1024
NT = (((1,), (1,)), ((), ()))

LON_LAT = ("lon", "lat")
SIDES = ((1, 0), (-1, 0), (1, 1), (1, -1), (-1, 1), (-1, -1))


def iota(shape, dim):
    return lax.broadcasted_iota(jnp.int32, shape, dim)


def remote(src, dst, send, recv, where):
    return pltpu.make_async_remote_copy(
        src_ref=src,
        dst_ref=dst,
        send_sem=send,
        recv_sem=recv,
        device_id=where,
        device_id_type=MESH_ID,
    )


def spot(lon, lat, mem):
    return {"lon": lon, "lat": lat, "mem": mem}


def row_of_all(stage, r, members):
    half = members * 16
    parts = [stage[pl.ds(h * half + r, members, stride=16), :] for h in range(2)]
    return jnp.concatenate(parts, axis=1)


def greet(places):
    barrier = pltpu.get_barrier_semaphore()
    for place in places:
        pl.semaphore_signal(barrier, inc=1, device_id=place, device_id_type=MESH_ID)
    return barrier, len(places)


def exchange_kernel(
    nlon,
    nlat,
    anom,
    mean,
    cx,
    cy,
    ocean,
    values,
    variance,
    cells,
    tile,
    count,
    lagged,
    from_north,
    from_south,
    beside,
    field_north,
    field_south,
    field_beside,
    arrived,
    lag_all,
    to_south,
    to_north,
    edges,
    fields,
    field_edges,
    placed,
    midway,
    turned,
    lag_near,
    stage,
    lag_sem,
    halo_send,
    halo_recv,
    lat_send,
    lat_recv,
    lon_send,
    lon_recv,
):
    lon, lat, mem = lax.axis_index("lon"), lax.axis_index("lat"), lax.axis_index("mem")

    def at(dx, dy):
        return spot(lax.rem(lon + dx + nlon, nlon), lax.rem(lat + dy + nlat, nlat), mem)

    peers = [at(0, d) for d in range(1, nlat)] + [at(d, 0) for d in range(1, nlon)]
    peers += [at(dx, dy) for dx, dy in SIDES if dy != 0]
    twin = spot(lon, lat, 1 - mem)
    barrier, total = greet(peers + [twin])
    load = pltpu.make_async_copy(lagged, lag_near, lag_sem.at[0])
    load.start()

    half = anom.shape[0] // 2
    sub = iota((half, 8, 256), 1)
    top = anom[:, 0:8, :].astype(F32)
    low = jnp.where(sub < 4, top[:half], pltpu.roll(top[half:], 4, 1))
    to_south[...] = low.astype(BF)
    bottom = anom[:, 8:16, :].astype(F32)
    high = jnp.where(sub < 4, pltpu.roll(bottom[:half], 4, 1), bottom[half:])
    to_north[...] = high.astype(BF)
    fields[0] = mean[...]
    fields[1] = cx[...]
    fields[2] = cy[...]
    fields[3] = ocean[...].astype(F32)

    lane = iota((16, 128), 1)

    def both_edges(x):
        return jnp.where(lane < 64, x[:, 0:128], x[:, 128:256])

    def packed(member, number):
        out = jnp.zeros((16, 128), F32)
        for k in range(number):
            moved = pltpu.roll(both_edges(member(k)), 8 * k, 1) if k else both_edges(member(k))
            mine = ((lane + 4) % 128) // 8 == k
            out = jnp.where(mine, moved, out)
        return out

    field_edges[...] = packed(lambda k: fields[k], 4)
    for g in range(anom.shape[0] // 16):
        edges[g] = packed(lambda k: anom[16 * g + k].astype(F32), 16).astype(BF)

    pl.semaphore_wait(barrier, total)

    copies = [
        remote(to_south, from_north, halo_send.at[0], halo_recv.at[0], at(0, -1)),
        remote(to_north, from_south, halo_send.at[1], halo_recv.at[1], at(0, 1)),
        remote(
            fields.at[:, 0:8, :], field_north, halo_send.at[2], halo_recv.at[2], at(0, -1)
        ),
        remote(
            fields.at[:, 8:16, :], field_south, halo_send.at[3], halo_recv.at[3], at(0, 1)
        ),
    ]
    for i, (dx, dy) in enumerate(SIDES):
        copies.append(
            remote(
                edges, beside.at[i], halo_send.at[4 + i], halo_recv.at[4 + i], at(-dx, -dy)
            )
        )
        copies.append(
            remote(
                field_edges,
                field_beside.at[i],
                halo_send.at[10 + i],
                halo_recv.at[10 + i],
                at(-dx, -dy),
            )
        )
    for copy in copies:
        copy.start()

    blocks, slots = values.shape
    row_i, col_i = iota((blocks, blocks), 0), iota((blocks, blocks), 1)
    same = row_i == col_i
    tile_col = jnp.broadcast_to(tile[...].astype(F32), (blocks, blocks))
    tile_row = jnp.sum(jnp.where(same, tile_col, 0.0), axis=0, keepdims=True)
    count_row = jnp.broadcast_to(count[...].astype(F32), (blocks, blocks))
    count_col = jnp.sum(jnp.where(same, count_row, 0.0), axis=1, keepdims=True)
    before = (tile_col == tile_row) & (row_i < col_i)
    rank = jnp.sum(jnp.where(before, 1.0, 0.0), axis=0, keepdims=True)
    wanted = (row_i % nlon) * nlat + row_i // nlon
    chosen = (wanted.astype(F32) == tile_row) & (rank == mem.astype(F32))
    selection = jnp.where(chosen, 1.0, 0.0).astype(BF)

    valid = iota((blocks, slots), 1).astype(F32) < count_col
    weight = jnp.where(valid, 1.0 / variance[...], 0.0)
    scaled = weight * values[...]
    where = cells[...]
    w_hi = weight.astype(BF).astype(F32)
    v_hi = scaled.astype(BF).astype(F32)
    payload = jnp.concatenate(
        [
            w_hi,
            weight - w_hi,
            v_hi,
            scaled - v_hi,
            (where // 256).astype(F32),
            (where % 256).astype(F32),
        ],
        axis=1,
    ).astype(BF)
    spread = jnp.dot(selection, payload, preferred_element_type=F32).astype(BF)
    placed[...] = spread.reshape(nlat, nlon, 6 * slots)

    first = []
    for d in range(1, nlat):
        to = lax.rem(lat + d, nlat)
        copy = remote(
            placed.at[to], midway.at[lat], lat_send.at[d - 1], lat_recv.at[d - 1], at(0, d)
        )
        copy.start()
        first.append(copy)
    midway[lat] = placed[lat]
    members = anom.shape[0]
    base = pl.multiple_of(mem * members, members)
    load.wait()
    for which in range(2):
        for h in range(2):
            part = lag_near[which, :, :, 128 * h : 128 * h + 128].astype(F32)
            stage[which, h * members * 16 : (h + 1) * members * 16] = part.reshape(-1, 128)
        for r in range(16):
            row = row_of_all(stage.at[which], r, members)
            lag_all[which, r, pl.ds(base, members), :] = row.astype(BF)
        copies.append(
            remote(
                lag_all.at[which, :, pl.ds(base, members), :],
                lag_all.at[which, :, pl.ds(base, members), :],
                halo_send.at[16 + which],
                halo_recv.at[16 + which],
                twin,
            )
        )
        copies[-1].start()
    for copy in first:
        copy.wait()

    swap = (row_i // nlat == col_i % nlon) & (row_i % nlat == col_i // nlon)
    mixed = midway[...].reshape(blocks, 6 * slots)
    ordered = jnp.dot(jnp.where(swap, 1.0, 0.0).astype(BF), mixed, preferred_element_type=F32)
    turned[...] = ordered.reshape(nlon, nlat, 6 * slots).astype(BF)
    second = []
    for d in range(1, nlon):
        to = lax.rem(lon + d, nlon)
        copy = remote(
            turned.at[to], arrived.at[lon], lon_send.at[d - 1], lon_recv.at[d - 1], at(d, 0)
        )
        copy.start()
        second.append(copy)
    arrived[lon] = turned[lon]
    for copy in second + copies:
        copy.wait()


def exchange(nlon, nlat, *args):
    members = args[0].shape[0]
    slots = args[5].shape[1]
    vm = pl.BlockSpec(memory_space=pltpu.VMEM)
    sds = jax.ShapeDtypeStruct
    lanes = 6 * slots
    return pl.pallas_call(
        functools.partial(exchange_kernel, nlon, nlat),
        out_shape=(
            sds((members // 2, 8, 256), BF),
            sds((members // 2, 8, 256), BF),
            sds((6, members // 16, 16, 128), BF),
            sds((4, 8, 256), F32),
            sds((4, 8, 256), F32),
            sds((6, 16, 128), F32),
            sds((nlon, nlat, lanes), BF),
            sds((2, 16, 2 * members, 256), BF),
        ),
        in_specs=[vm] * (len(args) - 1) + [pl.BlockSpec(memory_space=pl.ANY)],
        out_specs=(vm,) * 8,
        scratch_shapes=[
            pltpu.VMEM((members // 2, 8, 256), BF),
            pltpu.VMEM((members // 2, 8, 256), BF),
            pltpu.VMEM((members // 16, 16, 128), BF),
            pltpu.VMEM((4, 16, 256), F32),
            pltpu.VMEM((16, 128), F32),
            pltpu.VMEM((nlat, nlon, lanes), BF),
            pltpu.VMEM((nlat, nlon, lanes), BF),
            pltpu.VMEM((nlon, nlat, lanes), BF),
            pltpu.VMEM((2, members, 16, 256), BF),
            pltpu.VMEM((2, members * 32, 128), F32),
            pltpu.SemaphoreType.DMA((1,)),
            pltpu.SemaphoreType.DMA((18,)),
            pltpu.SemaphoreType.DMA((18,)),
            pltpu.SemaphoreType.DMA((nlat - 1,)),
            pltpu.SemaphoreType.DMA((nlat - 1,)),
            pltpu.SemaphoreType.DMA((nlon - 1,)),
            pltpu.SemaphoreType.DMA((nlon - 1,)),
        ],
        compiler_params=pltpu.CompilerParams(
            collective_id=0, has_side_effects=True, vmem_limit_bytes=LIMIT
        ),
        name="exchange",
    )(*args)


def forecast_kernel(
    nlat,
    anom,
    mean,
    cx,
    cy,
    ocean,
    from_north,
    from_south,
    beside,
    field_north,
    field_south,
    field_beside,
    arrived,
    rows_out,
    mean_out,
    cell_out,
    coef,
    side,
    stage,
    planes,
):
    lat = lax.axis_index("lat")
    members = anom.shape[0]
    half = members // 2
    north_ok = lat < nlat - 1
    south_ok = lat > 0
    lane16, sub8 = iota((16, 128), 1), iota((8, 128), 0)
    lane8 = iota((8, 128), 1)

    def sides(east, west, north_east, south_east, north_west, south_west):
        core = jnp.where(lane16 % 8 < 4, east, west)
        is_east = lane8 % 8 < 4
        up = jnp.where(is_east, north_east[0:8], north_west[0:8])
        down = jnp.where(is_east, south_east[8:16], south_west[8:16])
        up = jnp.where(north_ok, up, 0.0)
        down = jnp.where(south_ok, down, 0.0)
        return jnp.concatenate([core, jnp.where(sub8 < 4, up, down)], axis=0)

    for g in range(members // 16):
        side[g] = sides(*[beside[i, g].astype(F32) for i in range(6)])
    field_side = sides(*[field_beside[i] for i in range(6)])

    lane24 = iota((24, 128), 1)
    keep = (lane24 < 4) | (lane24 >= 124)
    subw = iota((8, 256), 0)

    def whole(core, up, down, turned):
        outer = jnp.where(subw < 4, jnp.where(north_ok, up, 0.0), jnp.where(south_ok, down, 0.0))
        return jnp.concatenate([jnp.concatenate([core, outer], axis=0), turned], axis=1)

    extended = []
    for k, core in enumerate((mean[...], cx[...], cy[...], ocean[...].astype(F32))):
        turned = pltpu.roll(field_side, 128 - 8 * k, 1) if k else field_side
        turned = jnp.where(keep, turned, 0.0)
        extended.append(whole(core, field_north[k], field_south[k], turned))
    ex_mean, ex_x, ex_y, ex_wet = extended
    coef[0] = ex_wet * jnp.maximum(ex_x, 0.0)
    coef[1] = -ex_wet * jnp.minimum(ex_x, 0.0)
    coef[2] = ex_wet * jnp.maximum(ex_y, 0.0)
    coef[3] = -ex_wet * jnp.minimum(ex_y, 0.0)

    def advance(q):
        for _ in range(SUBSTEPS):
            west = pltpu.roll(q, 1, 1)
            east = pltpu.roll(q, q.shape[1] - 1, 1)
            south = pltpu.roll(q, 1, 0)
            north = pltpu.roll(q, q.shape[0] - 1, 0)
            q = (
                q
                + coef[0] * (west - q)
                + coef[1] * (east - q)
                + coef[2] * (south - q)
                + coef[3] * (north - q)
            )
        return q[0:16, 0:256]

    mean_out[...] = advance(ex_mean)

    def one(i, carry):
        north, south = from_north[i].astype(F32), from_south[i].astype(F32)
        for second in (False, True):
            m = i + half if second else i
            up = pltpu.roll(north, 4, 0) if second else north
            down = south if second else pltpu.roll(south, 4, 0)
            turn = lax.rem(128 - 8 * lax.rem(i, 16), 128)
            turned = pltpu.roll(side[m // 16], turn, 1)
            q = whole(anom[m].astype(F32), up, down, turned)
            moved = advance(q)
            for h in range(2):
                start = pl.multiple_of((h * members + m) * 16, 16)
                stage[pl.ds(start, 16), :] = moved[:, 128 * h : 128 * h + 128]
        return carry

    lax.fori_loop(0, half, one, 0)
    for r in range(16):
        rows_out[r] = row_of_all(stage, r, members).astype(BF)

    lanes = arrived.shape[2]
    table = arrived[...].astype(F32).reshape(-1, lanes)
    count = table.shape[0] // 2
    first = iota((count, 128), 1) < 64
    for j in range(3):
        a = table[0:count, 128 * j : 128 * (j + 1)]
        b = table[count : 2 * count, 128 * j : 128 * (j + 1)]
        planes[2 * j] = jnp.where(first, a, pltpu.roll(b, 64, 1))
        planes[2 * j + 1] = jnp.where(first, pltpu.roll(a, 64, 1), b)
    row_id = iota((16, 256), 0).astype(F32)
    col_id = iota((256, 256), 0).astype(F32)

    def histogram(s, acc):
        def wide(p):
            return jnp.concatenate(
                [planes[p, pl.ds(2 * s, 1), :], planes[p, pl.ds(2 * s + 1, 1), :]], axis=1
            )

        hit = row_id == wide(4)
        left = jnp.concatenate([jnp.where(hit, wide(p), 0.0) for p in range(4)], axis=0)
        right = jnp.where(col_id == wide(5), 1.0, 0.0)
        return acc + lax.dot_general(
            left.astype(BF), right.astype(BF), NT, preferred_element_type=F32
        )

    acc = lax.fori_loop(0, count // 2, histogram, jnp.zeros((64, 256), F32))
    cell_out[0:16] = acc[0:16] + acc[16:32]
    cell_out[16:32] = acc[32:48] + acc[48:64]


def forecast(nlat, *args):
    members = args[0].shape[0]
    vm = pl.BlockSpec(memory_space=pltpu.VMEM)
    sds = jax.ShapeDtypeStruct
    return pl.pallas_call(
        functools.partial(forecast_kernel, nlat),
        out_shape=(
            sds((16, members, 256), BF),
            sds((16, 256), F32),
            sds((32, 256), F32),
        ),
        in_specs=[vm] * len(args),
        out_specs=(vm,) * 3,
        scratch_shapes=[
            pltpu.VMEM((4, 24, 384), F32),
            pltpu.VMEM((members // 16, 24, 128), F32),
            pltpu.VMEM((members * 32, 128), F32),
            pltpu.VMEM((6, 64, 128), F32),
        ],
        compiler_params=pltpu.CompilerParams(vmem_limit_bytes=LIMIT),
        name="forecast",
    )(*args)


def gram_kernel(
    nlon,
    nlat,
    own,
    cell,
    mean,
    everyone,
    gram,
    projection,
    cell_other,
    left,
    parts,
    got_lat,
    mine,
    got_lon,
    pair_send,
    pair_recv,
    lat_send,
    lat_recv,
    lon_send,
    lon_recv,
    all_send,
    all_recv,
):
    lon, lat, mem = lax.axis_index("lon"), lax.axis_index("lat"), lax.axis_index("mem")
    members = own.shape[1]
    base = pl.multiple_of(mem * members, members)
    twin = spot(lon, lat, 1 - mem)

    def at(dx, dy, m):
        return spot(lax.rem(lon + dx, nlon), lax.rem(lat + dy, nlat), m)

    across = [(d, m) for m in (0, 1) for d in range(nlat) if d or m]
    peers = [at(d, 0, mem) for d in range(1, nlon)]
    peers += [at(0, d, mem + m - 2 * mem * m) for d, m in across]
    barrier, total = greet(peers)
    everyone[:, pl.ds(base, members), :] = own[...]
    pl.semaphore_wait(barrier, total)

    pair = [
        remote(cell, cell_other, pair_send.at[0], pair_recv.at[0], twin),
        remote(
            own,
            everyone.at[:, pl.ds(base, members), :],
            pair_send.at[1],
            pair_recv.at[1],
            twin,
        ),
    ]
    for copy in pair:
        copy.start()
    pair[0].wait()
    sums = cell[...] + cell_other[...]
    weight = sums[0:16]
    misfit = sums[16:32] - weight * mean[...]
    for r in range(16):
        x = own[r].astype(F32)
        left[r, 0:members] = (x * weight[r : r + 1]).astype(BF)
        left[r, members : members + 16] = jnp.broadcast_to(misfit[r : r + 1], (16, 256)).astype(BF)
    pair[1].wait()
    acc = jnp.zeros((members + 16, 2 * members), F32)
    for r in range(16):
        acc = acc + lax.dot_general(left[r], everyone[r], NT, preferred_element_type=F32)
    for z in range(nlat):
        parts[z, 0:8] = acc[8 * z : 8 * z + 8]
        parts[z, 8:16] = acc[members : members + 8]

    first = []
    for d in range(1, nlat):
        to = lax.rem(lat + d, nlat)
        copy = remote(
            parts.at[to], got_lat.at[lat], lat_send.at[d - 1], lat_recv.at[d - 1], at(0, d, mem)
        )
        copy.start()
        first.append(copy)
    got_lat[lat] = parts[lat]
    for copy in first:
        copy.wait()
    part = got_lat[0]
    for z in range(1, nlat):
        part = part + got_lat[z]
    mine[...] = part

    second = []
    for d in range(1, nlon):
        copy = remote(mine, got_lon.at[lon], lon_send.at[d - 1], lon_recv.at[d - 1], at(d, 0, mem))
        copy.start()
        second.append(copy)
    got_lon[lon] = part
    for copy in second:
        copy.wait()
    part = got_lon[0]
    for x in range(1, nlon):
        part = part + got_lon[x]
    projection[...] = part[8:16]
    slot = mem * nlat + lat
    gram[slot] = part[0:8]
    third = []
    for i, (d, m) in enumerate(across):
        copy = remote(
            gram.at[slot],
            gram.at[slot],
            all_send.at[i],
            all_recv.at[i],
            at(0, d, mem + m - 2 * mem * m),
        )
        copy.start()
        third.append(copy)
    for copy in third:
        copy.wait()


def gram_sum(nlon, nlat, own, cell, mean):
    members = own.shape[1]
    vm = pl.BlockSpec(memory_space=pltpu.VMEM)
    sds = jax.ShapeDtypeStruct
    return pl.pallas_call(
        functools.partial(gram_kernel, nlon, nlat),
        out_shape=(
            sds((16, 2 * members, 256), BF),
            sds((2 * nlat, 8, 2 * members), F32),
            sds((8, 2 * members), F32),
        ),
        in_specs=[vm] * 3,
        out_specs=(vm,) * 3,
        scratch_shapes=[
            pltpu.VMEM((32, 256), F32),
            pltpu.VMEM((16, members + 16, 256), BF),
            pltpu.VMEM((nlat, 16, 2 * members), F32),
            pltpu.VMEM((nlat, 16, 2 * members), F32),
            pltpu.VMEM((16, 2 * members), F32),
            pltpu.VMEM((nlon, 16, 2 * members), F32),
            pltpu.SemaphoreType.DMA((2,)),
            pltpu.SemaphoreType.DMA((2,)),
            pltpu.SemaphoreType.DMA((nlat - 1,)),
            pltpu.SemaphoreType.DMA((nlat - 1,)),
            pltpu.SemaphoreType.DMA((nlon - 1,)),
            pltpu.SemaphoreType.DMA((nlon - 1,)),
            pltpu.SemaphoreType.DMA((2 * nlat - 1,)),
            pltpu.SemaphoreType.DMA((2 * nlat - 1,)),
        ],
        compiler_params=pltpu.CompilerParams(
            collective_id=1, has_side_effects=True, vmem_limit_bytes=LIMIT
        ),
        name="gram_sum",
    )(own, cell, mean)


def product(a, b):
    a_hi, b_hi = a.astype(BF), b.astype(BF)
    a_lo = (a - a_hi.astype(F32)).astype(BF)
    b_lo = (b - b_hi.astype(F32)).astype(BF)
    lhs = jnp.concatenate([a_hi, a_hi, a_lo], axis=1)
    rhs = jnp.concatenate([b_hi, b_lo, b_hi], axis=0)
    return jnp.dot(lhs, rhs, preferred_element_type=F32)


def inverse_root(gram, projection):
    n = gram.shape[0]
    identity = (iota((n, n), 0) == iota((n, n), 1)).astype(F32)
    system = (n - 1.0) * identity + 0.5 * (gram + gram.T)
    sums = jnp.sum(jnp.abs(system), axis=1, keepdims=True)
    bound = jnp.max(sums, axis=0, keepdims=True)
    iterate = system / bound
    factor = 1.5 * identity - 0.5 * iterate
    iterate = product(iterate, factor)
    accum = factor
    for _ in range(NS_ITERS - 2):
        factor = 1.5 * identity - 0.5 * product(accum, iterate)
        both = product(jnp.concatenate([iterate, accum], axis=0), factor)
        iterate, accum = both[0:n], both[n:]
    factor = 1.5 * identity - 0.5 * product(accum, iterate)
    root = product(factor, accum) / jnp.sqrt(bound)
    inner = jnp.sum(root * projection, axis=1, keepdims=True)
    weights = jnp.sum(root * inner, axis=0, keepdims=True)
    return root, weights


def analysis_kernel(
    gram,
    projection,
    now,
    lag,
    ocean,
    mean,
    lag_means,
    out,
    mean_out,
    transform,
    left,
    stage,
):
    step = pl.program_id(0)
    mem = lax.axis_index("mem")
    members = now.shape[1]
    own = members // 2
    base = pl.multiple_of(mem * own, own)

    @pl.when(step == 0)
    def _():
        n = members
        root, weights = inverse_root(gram[...].reshape(n, n), projection[0:1])
        transform[...] = jnp.sqrt(n - 1.0) * root
        left[0:own] = transform[pl.ds(base, own), :].astype(BF)
        left[own : own + 16] = jnp.broadcast_to(weights, (16, n)).astype(BF)

    wet = ocean[...].astype(F32)

    def update(x, own_x, r, mean_row):
        moved = jnp.dot(left[...], x, preferred_element_type=F32)
        s = own_x.astype(F32)
        w = wet[r : r + 1]
        blended = s + w * (moved[0:own] - s)
        for h in range(2):
            rows = pl.ds(h * own * 16 + r, own, stride=16)
            stage[rows, :] = blended[:, 128 * h : 128 * h + 128]
        mean_out[0, r : r + 1] = mean_row + w * moved[own : own + 1]

    @pl.when(step == 0)
    def _():
        for r in range(16):
            update(now[r], now[r, pl.ds(base, own), :], r, mean[r : r + 1])

    @pl.when(step > 0)
    def _():
        for r in range(16):
            update(lag[0, r], lag[0, r, pl.ds(base, own), :], r, lag_means[0, r : r + 1])

    for h in range(2):
        part = stage[h * own * 16 : (h + 1) * own * 16]
        out[0, :, :, 128 * h : 128 * h + 128] = part.reshape(own, 16, 128).astype(BF)


def analysis(gram, projection, now, lag, ocean, mean, lag_means):
    members = now.shape[1]
    own = members // 2
    vm = pl.BlockSpec(memory_space=pltpu.VMEM)
    sds = jax.ShapeDtypeStruct

    def lagged(s):
        return jnp.maximum(s - 1, 0)

    lag_spec = pl.BlockSpec((1, 16, members, 256), lambda s: (lagged(s), 0, 0, 0))
    return pl.pallas_call(
        analysis_kernel,
        grid=(3,),
        out_shape=(sds((3, own, 16, 256), BF), sds((3, 16, 256), F32)),
        in_specs=[vm, vm, vm, lag_spec, vm, vm]
        + [pl.BlockSpec((1, 16, 256), lambda s: (lagged(s), 0, 0))],
        out_specs=(
            pl.BlockSpec((1, own, 16, 256), lambda s: (s, 0, 0, 0)),
            pl.BlockSpec((1, 16, 256), lambda s: (s, 0, 0)),
        ),
        scratch_shapes=[
            pltpu.VMEM((members, members), F32),
            pltpu.VMEM((own + 16, members), BF),
            pltpu.VMEM((own * 32, 128), F32),
        ],
        compiler_params=pltpu.CompilerParams(vmem_limit_bytes=LIMIT),
        name="analysis",
    )(gram, projection, now, lag, ocean, mean, lag_means)


def body(
    nlon,
    nlat,
    anomalies,
    state_mean,
    delayed_deviation_pair,
    lagged_means,
    courant_lon,
    courant_lat,
    ocean,
    obs_values,
    obs_variance,
    obs_cells,
    obs_tile,
    obs_count,
):
    grids = (anomalies, state_mean, courant_lon, courant_lat, ocean)
    *halos, arrived, lag = exchange(
        nlon,
        nlat,
        *grids,
        obs_values,
        obs_variance,
        obs_cells,
        obs_tile,
        obs_count.reshape(1, -1),
        delayed_deviation_pair,
    )
    own, prior_mean, cell = forecast(nlat, *grids, *halos, arrived)
    now, gram, projection = gram_sum(nlon, nlat, own, cell, prior_mean)
    return analysis(gram, projection, now, lag, ocean, prior_mean, lagged_means)


def solution(mesh):
    return jax.shard_map(
        functools.partial(body, mesh.shape["lon"], mesh.shape["lat"]),
        mesh=mesh,
        in_specs=(
            P("mem", "lat", "lon"),
            P("lat", "lon"),
            P(None, "mem", "lat", "lon"),
            P(None, "lat", "lon"),
            P("lat", "lon"),
            P("lat", "lon"),
            P("lat", "lon"),
            P(LON_LAT, None),
            P(LON_LAT, None),
            P(LON_LAT, None),
            P(LON_LAT, None),
            P(LON_LAT),
        ),
        out_specs=(P(None, "mem", "lat", "lon"), P(None, "lat", "lon")),
        check_vma=False,
    )
```

```python
import functools

import jax
import jax.numpy as jnp
from jax import lax
from jax.experimental import pallas as pl
from jax.experimental.pallas import tpu as pltpu
from jax.sharding import PartitionSpec as P

SUBSTEPS = 4
NS_ITERS = 8
BF = jnp.bfloat16
F32 = jnp.float32
MESH_ID = pl.DeviceIdType.MESH
LIMIT = 48 * 1024 * 1024
NT = (((1,), (1,)), ((), ()))

LON_LAT = ("lon", "lat")
SIDES = ((1, 0), (-1, 0), (1, 1), (1, -1), (-1, 1), (-1, -1))


def iota(shape, dim):
    return lax.broadcasted_iota(jnp.int32, shape, dim)


def remote(src, dst, send, recv, where):
    return pltpu.make_async_remote_copy(
        src_ref=src,
        dst_ref=dst,
        send_sem=send,
        recv_sem=recv,
        device_id=where,
        device_id_type=MESH_ID,
    )


def spot(lon, lat, mem):
    return {"lon": lon, "lat": lat, "mem": mem}


def row_of_all(stage, r, members):
    half = members * 16
    parts = [stage[pl.ds(h * half + r, members, stride=16), :] for h in range(2)]
    return jnp.concatenate(parts, axis=1)


def greet(places):
    barrier = pltpu.get_barrier_semaphore()
    for place in places:
        pl.semaphore_signal(barrier, inc=1, device_id=place, device_id_type=MESH_ID)
    return barrier, len(places)


def smooth_kernel(
    nlon,
    nlat,
    anom_in,
    mean_in,
    cx_in,
    cy_in,
    ocean_in,
    values_in,
    variance_in,
    cells_in,
    tile_in,
    count_in,
    lagged_in,
    lag_means_in,
    everyone,
    gram,
    projection,
    mean_out,
    wet_out,
    lag_all,
    lag_means,
    anom,
    fields,
    ocean,
    values,
    variance,
    cells,
    tile,
    count,
    lag_near,
    to_south,
    to_north,
    edges,
    field_edges,
    from_north,
    from_south,
    beside,
    field_north,
    field_south,
    field_beside,
    placed,
    midway,
    turned,
    arrived,
    stage,
    coef,
    side,
    planes,
    cell,
    cell_other,
    left,
    parts,
    got_lat,
    mine,
    got_lon,
    load_sem,
    halo_send,
    halo_recv,
    chunk_send,
    chunk_recv,
    lat_send,
    lat_recv,
    lon_send,
    lon_recv,
    pair_send,
    pair_recv,
    sum_send,
    sum_recv,
    all_send,
    all_recv,
):
    lon, lat, mem = lax.axis_index("lon"), lax.axis_index("lat"), lax.axis_index("mem")
    twin = spot(lon, lat, 1 - mem)
    members = anom.shape[0]
    half = members // 2
    base = pl.multiple_of(mem * members, members)

    def at(dx, dy, m=mem):
        return spot(lax.rem(lon + dx + nlon, nlon), lax.rem(lat + dy + nlat, nlat), m)

    loads = [
        pltpu.make_async_copy(src, dst, load_sem.at[i])
        for i, (src, dst) in enumerate(
            (
                (anom_in, anom),
                (mean_in, fields.at[0]),
                (cx_in, fields.at[1]),
                (cy_in, fields.at[2]),
                (ocean_in, ocean),
                (tile_in, tile),
                (count_in, count),
                (values_in, values),
                (variance_in, variance),
                (cells_in, cells),
                (lagged_in, lag_near),
                (lag_means_in, lag_means),
            )
        )
    ]
    for load in loads:
        load.start()
    across = [(d, m) for m in (0, 1) for d in range(nlat) if d or m]

    def other(m):
        return mem + m - 2 * mem * m

    peers = [at(0, d, other(m)) for d, m in across]
    peers += [at(d, 0) for d in range(1, nlon)]
    peers += [at(dx, dy) for dx, dy in SIDES if dy != 0]
    barrier, total = greet(peers)

    for load in loads[:5]:
        load.wait()
    fields[3] = ocean[...].astype(F32)
    wet_out[...] = fields[3]
    sub = iota((half, 8, 256), 1)
    top = anom[:, 0:8, :].astype(F32)
    low = jnp.where(sub < 4, top[:half], pltpu.roll(top[half:], 4, 1))
    to_south[...] = low.astype(BF)
    bottom = anom[:, 8:16, :].astype(F32)
    high = jnp.where(sub < 4, pltpu.roll(bottom[:half], 4, 1), bottom[half:])
    to_north[...] = high.astype(BF)
    lane16 = iota((16, 128), 1)

    def both_edges(x):
        return jnp.where(lane16 < 64, x[:, 0:128], x[:, 128:256])

    def packed(member, number):
        out = jnp.zeros((16, 128), F32)
        for k in range(number):
            moved = pltpu.roll(both_edges(member(k)), 8 * k, 1) if k else both_edges(member(k))
            owner = ((lane16 + 4) % 128) // 8 == k
            out = jnp.where(owner, moved, out)
        return out

    field_edges[...] = packed(lambda k: fields[k], 4)
    for g in range(members // 16):
        edges[g] = packed(lambda k: anom[16 * g + k].astype(F32), 16).astype(BF)

    for load in loads[5:10]:
        load.wait()
    slots, blocks = values.shape
    row_i, col_i = iota((blocks, blocks), 0), iota((blocks, blocks), 1)
    tile_row = jnp.broadcast_to(tile[...].astype(F32), (blocks, blocks))
    tile_col = jnp.sum(jnp.where(row_i == col_i, tile_row, 0.0), axis=1, keepdims=True)
    before = (tile_col == tile_row) & (row_i < col_i)
    rank = jnp.sum(jnp.where(before, 1.0, 0.0), axis=0, keepdims=True)
    wanted = (row_i % nlon) * nlat + row_i // nlon
    chosen = (wanted.astype(F32) == tile_row) & (rank == mem.astype(F32))
    selection = jnp.where(chosen, 1.0, 0.0).astype(BF)
    valid = iota((slots, blocks), 0) < count[...]
    weight = jnp.where(valid, 1.0 / variance[...], 0.0)
    scaled = weight * values[...]
    where = cells[...]
    w_hi = weight.astype(BF).astype(F32)
    v_hi = scaled.astype(BF).astype(F32)
    payload = jnp.concatenate(
        [
            w_hi,
            weight - w_hi,
            v_hi,
            scaled - v_hi,
            (where // 256).astype(F32),
            (where % 256).astype(F32),
        ],
        axis=0,
    ).astype(BF)
    spread = lax.dot_general(selection, payload, NT, preferred_element_type=F32).astype(BF)
    placed[...] = spread.reshape(nlat, nlon, 6 * slots)

    pl.semaphore_wait(barrier, total)

    first = []
    for d in range(1, nlat):
        to = lax.rem(lat + d, nlat)
        first.append(
            remote(
                placed.at[to], midway.at[lat], lat_send.at[d - 1], lat_recv.at[d - 1], at(0, d)
            )
        )
    halo = []
    for i, (dx, dy) in enumerate(SIDES):
        there = at(-dx, -dy)
        halo.append(remote(edges, beside.at[i], halo_send.at[i], halo_recv.at[i], there))
        halo.append(
            remote(
                field_edges, field_beside.at[i], halo_send.at[6 + i], halo_recv.at[6 + i], there
            )
        )
    for j, (start, into, dy) in enumerate(((0, field_north, -1), (8, field_south, 1))):
        part = fields.at[:, pl.ds(start, 8), :]
        halo.append(remote(part, into, halo_send.at[12 + j], halo_recv.at[12 + j], at(0, dy)))
    chunks = 4
    wide_chunk = half // chunks
    bands = []
    for c in range(chunks):
        some = pl.ds(c * wide_chunk, wide_chunk)
        for j, (src, dst, dy) in enumerate(
            ((to_south, from_north, -1), (to_north, from_south, 1))
        ):
            k = 2 * c + j
            bands.append(
                remote(src.at[some], dst.at[some], chunk_send.at[k], chunk_recv.at[k], at(0, dy))
            )
    for copy in first + halo + bands:
        copy.start()
    midway[lat] = placed[lat]

    loads[10].wait()
    loads[11].wait()
    late = []
    for which in range(2):
        for h in range(2):
            part = lag_near[which, :, :, 128 * h : 128 * h + 128].astype(F32)
            stage[which, h * members * 16 : (h + 1) * members * 16] = part.reshape(-1, 128)
        for r in range(16):
            row = row_of_all(stage.at[which], r, members)
            lag_all[which, r, pl.ds(base, members), :] = row.astype(BF)
        ours = lag_all.at[which, :, pl.ds(base, members), :]
        late.append(remote(ours, ours, pair_send.at[5 + which], pair_recv.at[5 + which], twin))

    for copy in first:
        copy.wait()
    swap = (row_i // nlat == col_i % nlon) & (row_i % nlat == col_i // nlon)
    mixed = midway[...].reshape(blocks, 6 * slots)
    ordered = jnp.dot(jnp.where(swap, 1.0, 0.0).astype(BF), mixed, preferred_element_type=F32)
    turned[...] = ordered.reshape(nlon, nlat, 6 * slots).astype(BF)
    second = []
    for d in range(1, nlon):
        to = lax.rem(lon + d, nlon)
        copy = remote(
            turned.at[to], arrived.at[lon], lon_send.at[d - 1], lon_recv.at[d - 1], at(d, 0)
        )
        copy.start()
        second.append(copy)
    arrived[lon] = turned[lon]

    for copy in halo:
        copy.wait()
    north_ok = lat < nlat - 1
    south_ok = lat > 0
    sub8, lane8 = iota((8, 128), 0), iota((8, 128), 1)

    def sides(east, west, north_east, south_east, north_west, south_west):
        core = jnp.where(lane16 % 8 < 4, east, west)
        is_east = lane8 % 8 < 4
        up = jnp.where(is_east, north_east[0:8], north_west[0:8])
        down = jnp.where(is_east, south_east[8:16], south_west[8:16])
        up = jnp.where(north_ok, up, 0.0)
        down = jnp.where(south_ok, down, 0.0)
        return jnp.concatenate([core, jnp.where(sub8 < 4, up, down)], axis=0)

    for g in range(members // 16):
        side[g] = sides(*[beside[i, g].astype(F32) for i in range(6)])
    field_side = sides(*[field_beside[i] for i in range(6)])
    lane24 = iota((24, 128), 1)
    keep = (lane24 < 4) | (lane24 >= 124)
    subw = iota((8, 256), 0)

    def whole(core, up, down, turned):
        outer = jnp.where(subw < 4, jnp.where(north_ok, up, 0.0), jnp.where(south_ok, down, 0.0))
        return jnp.concatenate([jnp.concatenate([core, outer], axis=0), turned], axis=1)

    extended = []
    for k in range(4):
        turn = pltpu.roll(field_side, 128 - 8 * k, 1) if k else field_side
        turn = jnp.where(keep, turn, 0.0)
        extended.append(whole(fields[k], field_north[k], field_south[k], turn))
    ex_mean, ex_x, ex_y, ex_wet = extended
    coef[0] = ex_wet * jnp.maximum(ex_x, 0.0)
    coef[1] = -ex_wet * jnp.minimum(ex_x, 0.0)
    coef[2] = ex_wet * jnp.maximum(ex_y, 0.0)
    coef[3] = -ex_wet * jnp.minimum(ex_y, 0.0)
    coef[4] = 1.0 - ((coef[0] + coef[1]) + (coef[2] + coef[3]))

    def substep(q):
        west = pltpu.roll(q, 1, 1)
        east = pltpu.roll(q, q.shape[1] - 1, 1)
        south = pltpu.roll(q, 1, 0)
        north = pltpu.roll(q, q.shape[0] - 1, 0)
        return (coef[4] * q + coef[0] * west) + (coef[1] * east + coef[2] * south) + coef[3] * north

    q = ex_mean
    for _ in range(SUBSTEPS):
        q = substep(q)
    mean_out[...] = q[0:16, 0:256]
    together = 4

    def some_members(j, carry):
        where_to, group = [], []
        for k in range(together):
            i = j * together + k
            north, south = from_north[i].astype(F32), from_south[i].astype(F32)
            for second_half in (False, True):
                m = i + half if second_half else i
                up = pltpu.roll(north, 4, 0) if second_half else north
                down = south if second_half else pltpu.roll(south, 4, 0)
                turn = lax.rem(128 - 8 * lax.rem(i, 16), 128)
                turned_side = pltpu.roll(side[m // 16], turn, 1)
                where_to.append(m)
                group.append(whole(anom[m].astype(F32), up, down, turned_side))
        for _ in range(SUBSTEPS):
            group = [substep(q) for q in group]
        for m, q in zip(where_to, group):
            for h in range(2):
                start = pl.multiple_of((h * members + m) * 16, 16)
                stage[0, pl.ds(start, 16), :] = q[0:16, 128 * h : 128 * h + 128]
        return carry

    rounds = wide_chunk // together

    def advance(c):
        for copy in bands[2 * c : 2 * c + 2]:
            copy.wait()
        lax.fori_loop(c * rounds, (c + 1) * rounds, some_members, 0)

    for c in range(chunks - 1):
        advance(c)

    for copy in second:
        copy.wait()
    table = arrived[...].astype(F32).reshape(blocks, 6 * slots)
    pairs = blocks // 2
    near = iota((pairs, 128), 1) < 64
    for j in range(3):
        a = table[0:pairs, 128 * j : 128 * (j + 1)]
        b = table[pairs:blocks, 128 * j : 128 * (j + 1)]
        planes[2 * j] = jnp.where(near, a, pltpu.roll(b, 64, 1))
        planes[2 * j + 1] = jnp.where(near, pltpu.roll(a, 64, 1), b)
    row_id = iota((16, 256), 0).astype(F32)
    col_id = iota((256, 256), 0).astype(F32)

    def histogram(s, acc):
        def two(p):
            return jnp.concatenate(
                [planes[p, pl.ds(2 * s, 1), :], planes[p, pl.ds(2 * s + 1, 1), :]], axis=1
            )

        hit = row_id == two(4)
        lhs = jnp.concatenate([jnp.where(hit, two(p), 0.0) for p in range(4)], axis=0)
        rhs = jnp.where(col_id == two(5), 1.0, 0.0)
        return acc + lax.dot_general(lhs.astype(BF), rhs.astype(BF), NT, preferred_element_type=F32)

    acc = lax.fori_loop(0, pairs // 2, histogram, jnp.zeros((64, 256), F32), unroll=8)
    cell[0:16] = acc[0:16] + acc[16:32]
    cell[16:32] = acc[32:48] + acc[48:64]
    swap_cells = remote(cell, cell_other, pair_send.at[4], pair_recv.at[4], twin)
    swap_cells.start()

    advance(chunks - 1)

    swaps = []
    for c in range(4):
        for r in range(4 * c, 4 * c + 4):
            row = row_of_all(stage.at[0], r, members).astype(BF)
            everyone[r, pl.ds(base, members), :] = row
        ours = everyone.at[pl.ds(4 * c, 4), pl.ds(base, members), :]
        swaps.append(remote(ours, ours, pair_send.at[c], pair_recv.at[c], twin))
        swaps[-1].start()
    swap_cells.wait()
    sums = cell[...] + cell_other[...]
    weight = sums[0:16]
    misfit = sums[16:32] - weight * mean_out[...]
    for r in range(16):
        x = everyone[r, pl.ds(base, members), :].astype(F32)
        left[r, 0:members] = (x * weight[r : r + 1]).astype(BF)
        left[r, members : members + 16] = jnp.broadcast_to(misfit[r : r + 1], (16, 256)).astype(BF)
    acc = jnp.zeros((members + 16, 2 * members), F32)
    for c in range(4):
        swaps[c].wait()
        for r in range(4 * c, 4 * c + 4):
            acc = acc + lax.dot_general(left[r], everyone[r], NT, preferred_element_type=F32)
    for z in range(nlat):
        parts[z, 0:8] = acc[8 * z : 8 * z + 8]
        parts[z, 8:9] = acc[members : members + 1]

    first = []
    for d in range(1, nlat):
        to = lax.rem(lat + d, nlat)
        k = d - 1
        copy = remote(parts.at[to], got_lat.at[lat], sum_send.at[k], sum_recv.at[k], at(0, d))
        copy.start()
        first.append(copy)
    got_lat[lat] = parts[lat]
    for copy in late:
        copy.start()
    for copy in first:
        copy.wait()
    part = got_lat[0]
    for z in range(1, nlat):
        part = part + got_lat[z]
    mine[...] = part

    second = []
    for d in range(1, nlon):
        k = nlat + d - 2
        copy = remote(mine, got_lon.at[lon], sum_send.at[k], sum_recv.at[k], at(d, 0))
        copy.start()
        second.append(copy)
    got_lon[lon] = part
    for copy in second:
        copy.wait()
    part = got_lon[0]
    for x in range(1, nlon):
        part = part + got_lon[x]
    projection[...] = jnp.broadcast_to(part[8:9], projection.shape)
    slot = mem * nlat + lat
    gram[slot] = part[0:8]
    third = []
    for i, (d, m) in enumerate(across):
        copy = remote(
            gram.at[slot], gram.at[slot], all_send.at[i], all_recv.at[i], at(0, d, other(m))
        )
        copy.start()
        third.append(copy)
    for copy in third + late:
        copy.wait()


def smooth(nlon, nlat, *args):
    members = args[0].shape[0]
    slots, blocks = args[5].shape
    vm = pl.BlockSpec(memory_space=pltpu.VMEM)
    sds = jax.ShapeDtypeStruct
    lanes = 6 * slots
    pair = 2 * members
    dma = pltpu.SemaphoreType.DMA
    return pl.pallas_call(
        functools.partial(smooth_kernel, nlon, nlat),
        out_shape=(
            sds((16, pair, 256), BF),
            sds((2 * nlat, 8, pair), F32),
            sds((8, pair), F32),
            sds((16, 256), F32),
            sds((16, 256), F32),
            sds((2, 16, pair, 256), BF),
            sds((2, 16, 256), F32),
        ),
        in_specs=[pl.BlockSpec(memory_space=pltpu.MemorySpace.HBM)] * len(args),
        out_specs=(vm,) * 7,
        scratch_shapes=[
            pltpu.VMEM((members, 16, 256), BF),
            pltpu.VMEM((4, 16, 256), F32),
            pltpu.VMEM((16, 256), jnp.int32),
            pltpu.VMEM((slots, blocks), F32),
            pltpu.VMEM((slots, blocks), F32),
            pltpu.VMEM((slots, blocks), jnp.int32),
            pltpu.VMEM((1, blocks), jnp.int32),
            pltpu.VMEM((1, blocks), jnp.int32),
            pltpu.VMEM((2, members, 16, 256), BF),
            pltpu.VMEM((members // 2, 8, 256), BF),
            pltpu.VMEM((members // 2, 8, 256), BF),
            pltpu.VMEM((members // 16, 16, 128), BF),
            pltpu.VMEM((16, 128), F32),
            pltpu.VMEM((members // 2, 8, 256), BF),
            pltpu.VMEM((members // 2, 8, 256), BF),
            pltpu.VMEM((6, members // 16, 16, 128), BF),
            pltpu.VMEM((4, 8, 256), F32),
            pltpu.VMEM((4, 8, 256), F32),
            pltpu.VMEM((6, 16, 128), F32),
            pltpu.VMEM((nlat, nlon, lanes), BF),
            pltpu.VMEM((nlat, nlon, lanes), BF),
            pltpu.VMEM((nlon, nlat, lanes), BF),
            pltpu.VMEM((nlon, nlat, lanes), BF),
            pltpu.VMEM((2, members * 32, 128), F32),
            pltpu.VMEM((5, 24, 384), F32),
            pltpu.VMEM((members // 16, 24, 128), F32),
            pltpu.VMEM((6, blocks // 2, 128), F32),
            pltpu.VMEM((32, 256), F32),
            pltpu.VMEM((32, 256), F32),
            pltpu.VMEM((16, members + 16, 256), BF),
            pltpu.VMEM((nlat, 9, pair), F32),
            pltpu.VMEM((nlat, 9, pair), F32),
            pltpu.VMEM((9, pair), F32),
            pltpu.VMEM((nlon, 9, pair), F32),
            dma((12,)),
            dma((14,)),
            dma((14,)),
            dma((8,)),
            dma((8,)),
            dma((nlat - 1,)),
            dma((nlat - 1,)),
            dma((nlon - 1,)),
            dma((nlon - 1,)),
            dma((7,)),
            dma((7,)),
            dma((nlon + nlat - 2,)),
            dma((nlon + nlat - 2,)),
            dma((2 * nlat - 1,)),
            dma((2 * nlat - 1,)),
        ],
        compiler_params=pltpu.CompilerParams(
            collective_id=0, has_side_effects=True, vmem_limit_bytes=LIMIT
        ),
        name="smooth",
    )(*[pltpu.with_memory_space_constraint(a, pltpu.MemorySpace.HBM) for a in args])


def product(a, b):
    a_hi, b_hi = a.astype(BF), b.astype(BF)
    a_lo = (a - a_hi.astype(F32)).astype(BF)
    b_lo = (b - b_hi.astype(F32)).astype(BF)
    lhs = jnp.concatenate([a_hi, a_hi, a_lo], axis=1)
    rhs = jnp.concatenate([b_hi, b_lo, b_hi], axis=0)
    return jnp.dot(lhs, rhs, preferred_element_type=F32)


def inverse_root(gram, projection):
    n = gram.shape[0]
    identity = (iota((n, n), 0) == iota((n, n), 1)).astype(F32)
    system = (n - 1.0) * identity + 0.5 * (gram + gram.T)
    sums = jnp.sum(jnp.abs(system), axis=1, keepdims=True)
    bound = jnp.max(sums, axis=0, keepdims=True)
    iterate = system / bound
    factor = 1.5 * identity - 0.5 * iterate
    iterate = product(iterate, factor)
    accum = factor
    for _ in range(NS_ITERS - 2):
        factor = 1.5 * identity - 0.5 * product(accum, iterate)
        both = product(jnp.concatenate([iterate, accum], axis=0), factor)
        iterate, accum = both[0:n], both[n:]
    factor = 1.5 * identity - 0.5 * product(accum, iterate)
    root = product(factor, accum) / jnp.sqrt(bound)
    inner = jnp.sum(root * projection, axis=1, keepdims=True)
    weights = jnp.sum(root * inner, axis=0, keepdims=True)
    return root, weights


def analysis_kernel(
    gram,
    projection,
    now,
    lag,
    ocean,
    mean,
    lag_means,
    out,
    mean_out,
    transform,
    left,
    stage,
):
    step = pl.program_id(0)
    mem = lax.axis_index("mem")
    members = now.shape[1]
    own = members // 2
    base = pl.multiple_of(mem * own, own)

    @pl.when(step == 0)
    def _():
        n = members
        root, weights = inverse_root(gram[...].reshape(n, n), projection[0:1])
        transform[...] = jnp.sqrt(n - 1.0) * root
        left[0:own] = transform[pl.ds(base, own), :].astype(BF)
        left[own : own + 16] = jnp.broadcast_to(weights, (16, n)).astype(BF)

    wet = ocean[...]

    def update(x, own_x, r, mean_row):
        moved = jnp.dot(left[...], x, preferred_element_type=F32)
        s = own_x.astype(F32)
        w = wet[r : r + 1]
        blended = s + w * (moved[0:own] - s)
        for h in range(2):
            rows = pl.ds(h * own * 16 + r, own, stride=16)
            stage[rows, :] = blended[:, 128 * h : 128 * h + 128]
        mean_out[0, r : r + 1] = mean_row + w * moved[own : own + 1]

    @pl.when(step == 0)
    def _():
        for r in range(16):
            update(now[r], now[r, pl.ds(base, own), :], r, mean[r : r + 1])

    @pl.when(step > 0)
    def _():
        for r in range(16):
            update(lag[0, r], lag[0, r, pl.ds(base, own), :], r, lag_means[0, r : r + 1])

    for h in range(2):
        part = stage[h * own * 16 : (h + 1) * own * 16]
        out[0, :, :, 128 * h : 128 * h + 128] = part.reshape(own, 16, 128).astype(BF)


def analysis(gram, projection, now, lag, ocean, mean, lag_means):
    members = now.shape[1]
    own = members // 2
    vm = pl.BlockSpec(memory_space=pltpu.VMEM)
    sds = jax.ShapeDtypeStruct

    def lagged(s):
        return jnp.maximum(s - 1, 0)

    lag_spec = pl.BlockSpec((1, 16, members, 256), lambda s: (lagged(s), 0, 0, 0))
    return pl.pallas_call(
        analysis_kernel,
        grid=(3,),
        out_shape=(sds((3, own, 16, 256), BF), sds((3, 16, 256), F32)),
        in_specs=[vm, vm, vm, lag_spec, vm, vm]
        + [pl.BlockSpec((1, 16, 256), lambda s: (lagged(s), 0, 0))],
        out_specs=(
            pl.BlockSpec((1, own, 16, 256), lambda s: (s, 0, 0, 0)),
            pl.BlockSpec((1, 16, 256), lambda s: (s, 0, 0)),
        ),
        scratch_shapes=[
            pltpu.VMEM((members, members), F32),
            pltpu.VMEM((own + 16, members), BF),
            pltpu.VMEM((own * 32, 128), F32),
        ],
        compiler_params=pltpu.CompilerParams(vmem_limit_bytes=LIMIT),
        name="analysis",
    )(gram, projection, now, lag, ocean, mean, lag_means)


def body(
    nlon,
    nlat,
    anomalies,
    state_mean,
    delayed_deviation_pair,
    lagged_means,
    courant_lon,
    courant_lat,
    ocean,
    obs_values,
    obs_variance,
    obs_cells,
    obs_tile,
    obs_count,
):
    now, gram, projection, prior_mean, wet, lag, lag_means = smooth(
        nlon,
        nlat,
        anomalies,
        state_mean,
        courant_lon,
        courant_lat,
        ocean,
        obs_values.T,
        obs_variance.T,
        obs_cells.T,
        obs_tile.reshape(1, -1),
        obs_count.reshape(1, -1),
        delayed_deviation_pair,
        lagged_means,
    )
    return analysis(gram, projection, now, lag, wet, prior_mean, lag_means)


def solution(mesh):
    return jax.shard_map(
        functools.partial(body, mesh.shape["lon"], mesh.shape["lat"]),
        mesh=mesh,
        in_specs=(
            P("mem", "lat", "lon"),
            P("lat", "lon"),
            P(None, "mem", "lat", "lon"),
            P(None, "lat", "lon"),
            P("lat", "lon"),
            P("lat", "lon"),
            P("lat", "lon"),
            P(LON_LAT, None),
            P(LON_LAT, None),
            P(LON_LAT, None),
            P(LON_LAT, None),
            P(LON_LAT),
        ),
        out_specs=(P(None, "mem", "lat", "lon"), P(None, "lat", "lon")),
        check_vma=False,
    )
```

```python
import functools

import jax
import jax.numpy as jnp
from jax import lax
from jax.experimental import pallas as pl
from jax.experimental.pallas import tpu as pltpu
from jax.sharding import PartitionSpec as P

SUBSTEPS = 4
NS_ITERS = 8
BF = jnp.bfloat16
F32 = jnp.float32
MESH_ID = pl.DeviceIdType.MESH
LIMIT = 48 * 1024 * 1024
NT = (((1,), (1,)), ((), ()))

LON_LAT = ("lon", "lat")
SIDES = ((1, 0), (-1, 0), (1, 1), (1, -1), (-1, 1), (-1, -1))


def iota(shape, dim):
    return lax.broadcasted_iota(jnp.int32, shape, dim)


def remote(src, dst, send, recv, where):
    return pltpu.make_async_remote_copy(
        src_ref=src,
        dst_ref=dst,
        send_sem=send,
        recv_sem=recv,
        device_id=where,
        device_id_type=MESH_ID,
    )


def spot(lon, lat, mem):
    return {"lon": lon, "lat": lat, "mem": mem}


def row_of_all(stage, r, members):
    half = members * 16
    parts = [stage[pl.ds(h * half + r, members, stride=16), :] for h in range(2)]
    return jnp.concatenate(parts, axis=1)


def greet(places):
    barrier = pltpu.get_barrier_semaphore()
    for place in places:
        pl.semaphore_signal(barrier, inc=1, device_id=place, device_id_type=MESH_ID)
    return barrier, len(places)


def smooth_kernel(
    nlon,
    nlat,
    anom_in,
    mean_in,
    cx_in,
    cy_in,
    ocean_in,
    values_in,
    variance_in,
    cells_in,
    tile_in,
    count_in,
    lagged_in,
    lag_means_in,
    everyone,
    gram,
    projection,
    mean_out,
    wet_out,
    lag_all,
    lag_means,
    anom,
    fields,
    ocean,
    values,
    variance,
    cells,
    tile,
    count,
    lag_near,
    to_south,
    to_north,
    edges,
    corners,
    field_edges,
    field_corner,
    field_south_out,
    field_north_out,
    from_north,
    from_south,
    beside,
    beyond,
    field_north,
    field_south,
    field_beside,
    field_beyond,
    placed,
    midway,
    turned,
    arrived,
    stage,
    coef,
    side,
    planes,
    cell,
    cell_other,
    left,
    parts,
    got_lat,
    mine,
    got_lon,
    load_sem,
    halo_send,
    halo_recv,
    chunk_send,
    chunk_recv,
    lat_send,
    lat_recv,
    lon_send,
    lon_recv,
    pair_send,
    pair_recv,
    sum_send,
    sum_recv,
    all_send,
    all_recv,
):
    lon, lat, mem = lax.axis_index("lon"), lax.axis_index("lat"), lax.axis_index("mem")
    twin = spot(lon, lat, 1 - mem)
    members = anom.shape[0]
    base = pl.multiple_of(mem * members, members)

    def at(dx, dy, m=mem):
        return spot(lax.rem(lon + dx + nlon, nlon), lax.rem(lat + dy + nlat, nlat), m)

    loads = [
        pltpu.make_async_copy(src, dst, load_sem.at[i])
        for i, (src, dst) in enumerate(
            (
                (anom_in, anom),
                (mean_in, fields.at[0]),
                (cx_in, fields.at[1]),
                (cy_in, fields.at[2]),
                (ocean_in, ocean),
                (tile_in, tile),
                (count_in, count),
                (values_in, values),
                (variance_in, variance),
                (cells_in, cells),
                (lagged_in, lag_near),
                (lag_means_in, lag_means),
            )
        )
    ]
    for load in loads:
        load.start()
    across = [(d, m) for m in (0, 1) for d in range(nlat) if d or m]

    def other(m):
        return mem + m - 2 * mem * m

    peers = [at(0, d, other(m)) for d, m in across]
    peers += [at(d, 0) for d in range(1, nlon)]
    peers += [at(dx, dy) for dx, dy in SIDES if dy != 0]
    barrier, total = greet(peers)

    for load in loads[:5]:
        load.wait()
    fields[3] = ocean[...].astype(F32)
    wet_out[...] = fields[3]
    chunks = members // 16

    def banded(x, above):
        low, high = x[:, : x.shape[1] // 2], x[:, x.shape[1] // 2 :]
        if above:
            low = pltpu.roll(low, 4, 2)
        else:
            high = pltpu.roll(high, 4, 2)
        return jnp.where(iota(low.shape, 2) < 4, low, high)

    top = anom[:, 0:8, :].astype(F32).reshape(chunks, 16, 8, 256)
    to_south[...] = banded(top, False).astype(BF)
    bottom = anom[:, 8:16, :].astype(F32).reshape(chunks, 16, 8, 256)
    to_north[...] = banded(bottom, True).astype(BF)
    field_south_out[...] = banded(fields[:, 0:8, :].reshape(1, 4, 8, 256), False)[0]
    field_north_out[...] = banded(fields[:, 8:16, :].reshape(1, 4, 8, 256), True)[0]
    lane16 = iota((16, 128), 1)

    def both_edges(x):
        return jnp.where(lane16 < 64, x[:, 0:128], x[:, 128:256])

    def packed(member, number):
        out = jnp.zeros((16, 128), F32)
        for k in range(number):
            moved = pltpu.roll(both_edges(member(k)), 8 * k, 1) if k else both_edges(member(k))
            owner = ((lane16 + 4) % 128) // 8 == k
            out = jnp.where(owner, moved, out)
        return out

    sub8, lane8 = iota((8, 128), 0), iota((8, 128), 1)

    def corner(x):
        return jnp.where(sub8 < 4, x[0:8], x[8:16])

    packed_fields = packed(lambda k: fields[k], 4)
    field_edges[...] = packed_fields
    field_corner[...] = corner(packed_fields)
    for g in range(chunks):
        packed_group = packed(lambda k: anom[16 * g + k].astype(F32), 16)
        edges[g] = packed_group.astype(BF)
        corners[g] = corner(packed_group).astype(BF)

    for load in loads[5:10]:
        load.wait()
    slots, blocks = values.shape
    row_i, col_i = iota((blocks, blocks), 0), iota((blocks, blocks), 1)
    tile_row = jnp.broadcast_to(tile[...].astype(F32), (blocks, blocks))
    tile_col = jnp.sum(jnp.where(row_i == col_i, tile_row, 0.0), axis=1, keepdims=True)
    before = (tile_col == tile_row) & (row_i < col_i)
    rank = jnp.sum(jnp.where(before, 1.0, 0.0), axis=0, keepdims=True)
    chosen = (row_i.astype(F32) == tile_row) & (rank == mem.astype(F32))
    selection = jnp.where(chosen, 1.0, 0.0).astype(BF)
    valid = iota((slots, blocks), 0) < count[...]
    weight = jnp.where(valid, 1.0 / variance[...], 0.0)
    scaled = weight * values[...]
    where = cells[...]
    w_hi = weight.astype(BF).astype(F32)
    v_hi = scaled.astype(BF).astype(F32)
    payload = jnp.concatenate(
        [
            w_hi,
            weight - w_hi,
            v_hi,
            scaled - v_hi,
            (where // 256).astype(F32),
            (where % 256).astype(F32),
        ],
        axis=0,
    ).astype(BF)
    spread = lax.dot_general(selection, payload, NT, preferred_element_type=F32)
    placed[...] = spread.reshape(nlon, nlat, 6 * slots).astype(BF)

    pl.semaphore_wait(barrier, total)

    first = []
    for d in range(1, nlon):
        to = lax.rem(lon + d, nlon)
        k = d - 1
        first.append(
            remote(placed.at[to], midway.at[lon], lon_send.at[k], lon_recv.at[k], at(d, 0))
        )
    halo = []
    pieces = [(field_south_out, field_north, 0, -1), (field_north_out, field_south, 0, 1)]
    for i, (dx, dy) in enumerate(SIDES[:2]):
        pieces.append((edges, beside.at[i], -dx, -dy))
        pieces.append((field_edges, field_beside.at[i], -dx, -dy))
    for i, (dx, dy) in enumerate(SIDES[2:]):
        pieces.append((corners, beyond.at[i], -dx, -dy))
        pieces.append((field_corner, field_beyond.at[i], -dx, -dy))
    for i, (src, dst, dx, dy) in enumerate(pieces):
        halo.append(remote(src, dst, halo_send.at[i], halo_recv.at[i], at(dx, dy)))
    bands = []
    for c in range(chunks):
        for j, (src, dst, dy) in enumerate(
            ((to_south, from_north, -1), (to_north, from_south, 1))
        ):
            k = 2 * c + j
            bands.append(
                remote(src.at[c], dst.at[c], chunk_send.at[k], chunk_recv.at[k], at(0, dy))
            )
    for copy in halo + bands[:2] + first + bands[2:]:
        copy.start()
    midway[lon] = placed[lon]

    loads[10].wait()
    loads[11].wait()
    late = []
    for which in range(2):
        for h in range(2):
            part = lag_near[which, :, :, 128 * h : 128 * h + 128].astype(F32)
            stage[which, h * members * 16 : (h + 1) * members * 16] = part.reshape(-1, 128)
        for r in range(16):
            row = row_of_all(stage.at[which], r, members)
            lag_all[which, r, pl.ds(base, members), :] = row.astype(BF)
        ours = lag_all.at[which, :, pl.ds(base, members), :]
        late.append(remote(ours, ours, pair_send.at[5 + which], pair_recv.at[5 + which], twin))
        late[-1].start()

    for copy in first:
        copy.wait()
    swap = (row_i // nlon == col_i % nlat) & (row_i % nlon == col_i // nlat)
    mixed = midway[...].astype(F32).reshape(blocks, 6 * slots).astype(BF)
    ordered = jnp.dot(jnp.where(swap, 1.0, 0.0).astype(BF), mixed, preferred_element_type=F32)
    turned[...] = ordered.reshape(nlat, nlon, 6 * slots).astype(BF)
    second = []
    for d in range(1, nlat):
        to = lax.rem(lat + d, nlat)
        copy = remote(
            turned.at[to], arrived.at[lat], lat_send.at[d - 1], lat_recv.at[d - 1], at(0, d)
        )
        copy.start()
        second.append(copy)
    arrived[lat] = turned[lat]
    for copy in halo:
        copy.wait()
    north_ok = lat < nlat - 1
    south_ok = lat > 0

    def sides(east, west, north_east, south_east, north_west, south_west):
        core = jnp.where(lane16 % 8 < 4, east, west)
        is_east = lane8 % 8 < 4
        up = jnp.where(is_east, north_east, north_west)
        down = jnp.where(is_east, south_east, south_west)
        up = jnp.where(north_ok, up, 0.0)
        down = jnp.where(south_ok, down, 0.0)
        return jnp.concatenate([core, jnp.where(sub8 < 4, up, down)], axis=0)

    for g in range(chunks):
        near = [beside[i, g].astype(F32) for i in range(2)]
        side[g] = sides(*near, *[beyond[i, g].astype(F32) for i in range(4)])
    field_side = sides(*[field_beside[i] for i in range(2)], *[field_beyond[i] for i in range(4)])
    lane24 = iota((24, 128), 1)
    keep = (lane24 < 4) | (lane24 >= 124)
    subw = iota((8, 256), 0)

    def whole(core, up, down, turned):
        outer = jnp.where(subw < 4, jnp.where(north_ok, up, 0.0), jnp.where(south_ok, down, 0.0))
        return jnp.concatenate([jnp.concatenate([core, outer], axis=0), turned], axis=1)

    extended = []
    for k in range(4):
        turn = pltpu.roll(field_side, 128 - 8 * k, 1) if k else field_side
        turn = jnp.where(keep, turn, 0.0)
        up, down = field_north[k % 2], field_south[k % 2]
        if k < 2:
            down = pltpu.roll(down, 4, 0)
        else:
            up = pltpu.roll(up, 4, 0)
        extended.append(whole(fields[k], up, down, turn))
    ex_mean, ex_x, ex_y, ex_wet = extended
    coef[0] = ex_wet * jnp.maximum(ex_x, 0.0)
    coef[1] = -ex_wet * jnp.minimum(ex_x, 0.0)
    coef[2] = ex_wet * jnp.maximum(ex_y, 0.0)
    coef[3] = -ex_wet * jnp.minimum(ex_y, 0.0)
    coef[4] = 1.0 - ((coef[0] + coef[1]) + (coef[2] + coef[3]))

    def substep(q):
        west = pltpu.roll(q, 1, 1)
        east = pltpu.roll(q, q.shape[1] - 1, 1)
        south = pltpu.roll(q, 1, 0)
        north = pltpu.roll(q, q.shape[0] - 1, 0)
        return (coef[4] * q + coef[0] * west) + (coef[1] * east + coef[2] * south) + coef[3] * north

    swaps = []

    def advance(c):
        for copy in bands[2 * c : 2 * c + 2]:
            copy.wait()
        where_to, group = [], []
        for i in range(8):
            north, south = from_north[c, i].astype(F32), from_south[c, i].astype(F32)
            for later in (0, 8):
                m = 16 * c + i + later
                up = pltpu.roll(north, 4, 0) if later else north
                down = south if later else pltpu.roll(south, 4, 0)
                turn = (128 - 8 * (i + later)) % 128
                turned_side = pltpu.roll(side[c], turn, 1) if turn else side[c]
                where_to.append(m)
                group.append(whole(anom[m].astype(F32), up, down, turned_side))
        if c == 0:
            group.append(ex_mean)
        for _ in range(SUBSTEPS):
            group = [substep(q) for q in group]
        if c == 0:
            mean_out[...] = group.pop()[0:16, 0:256]
        for m, q in zip(where_to, group):
            for h in range(2):
                start = (h * members + m) * 16
                stage[0, start : start + 16, :] = q[0:16, 128 * h : 128 * h + 128]
        rows = pl.ds(pl.multiple_of(base + 16 * c, 16), 16)
        for r in range(16):
            parts_of_row = [
                stage[0, pl.ds((h * members + 16 * c) * 16 + r, 16, stride=16), :]
                for h in range(2)
            ]
            everyone[r, rows, :] = jnp.concatenate(parts_of_row, axis=1).astype(BF)
        ours = everyone.at[:, rows, :]
        swaps.append(remote(ours, ours, pair_send.at[c], pair_recv.at[c], twin))
        swaps[-1].start()

    advance(0)
    for c in range(1, chunks - 1):
        advance(c)

    advance(chunks - 1)

    for copy in second:
        copy.wait()
    table = arrived[...].astype(F32).reshape(blocks, 6 * slots)
    pairs = blocks // 2
    near = iota((pairs, 128), 1) < 64
    for j in range(3):
        a = table[0:pairs, 128 * j : 128 * (j + 1)]
        b = table[pairs:blocks, 128 * j : 128 * (j + 1)]
        planes[2 * j] = jnp.where(near, a, pltpu.roll(b, 64, 1))
        planes[2 * j + 1] = jnp.where(near, pltpu.roll(a, 64, 1), b)
    row_id = iota((16, 256), 0).astype(F32)
    col_id = iota((256, 256), 0).astype(F32)

    def histogram(s, acc):
        def two(p):
            return jnp.concatenate(
                [planes[p, pl.ds(2 * s, 1), :], planes[p, pl.ds(2 * s + 1, 1), :]], axis=1
            )

        hit = row_id == two(4)
        lhs = jnp.concatenate([jnp.where(hit, two(p), 0.0) for p in range(4)], axis=0)
        rhs = jnp.where(col_id == two(5), 1.0, 0.0)
        return acc + lax.dot_general(lhs.astype(BF), rhs.astype(BF), NT, preferred_element_type=F32)

    acc = lax.fori_loop(0, pairs // 2, histogram, jnp.zeros((64, 256), F32), unroll=8)
    cell[0:16] = acc[0:16] + acc[16:32]
    cell[16:32] = acc[32:48] + acc[48:64]
    swap_cells = remote(cell, cell_other, pair_send.at[4], pair_recv.at[4], twin)
    swap_cells.start()


    swap_cells.wait()
    sums = cell[...] + cell_other[...]
    weight = sums[0:16]
    misfit = sums[16:32] - weight * mean_out[...]
    for r in range(16):
        x = everyone[r, pl.ds(base, members), :].astype(F32)
        left[r, 0:members] = (x * weight[r : r + 1]).astype(BF)
        left[r, members : members + 16] = jnp.broadcast_to(misfit[r : r + 1], (16, 256)).astype(BF)
    acc = jnp.zeros((members + 16, 2 * members), F32)
    for copy in swaps:
        copy.wait()
    for r in range(16):
        acc = acc + lax.dot_general(left[r], everyone[r], NT, preferred_element_type=F32)
    own = members // nlon
    for x in range(nlon):
        parts[x, 0:own] = acc[own * x : own * x + own]
        parts[x, own : own + 1] = acc[members : members + 1]

    first = []
    for d in range(1, nlon):
        to = lax.rem(lon + d, nlon)
        k = d - 1
        copy = remote(parts.at[to], got_lon.at[lon], sum_send.at[k], sum_recv.at[k], at(d, 0))
        copy.start()
        first.append(copy)
    got_lon[lon] = parts[lon]
    for copy in first:
        copy.wait()
    part = got_lon[0]
    for x in range(1, nlon):
        part = part + got_lon[x]
    mine[...] = part

    second = []
    for i, (d, m) in enumerate(across):
        copy = remote(
            mine, got_lat.at[mem, lat], all_send.at[i], all_recv.at[i], at(0, d, other(m))
        )
        copy.start()
        second.append(copy)
    got_lat[mem, lat] = part
    for copy in second:
        copy.wait()
    totals = []
    for m in range(2):
        part = got_lat[m, 0]
        for z in range(1, nlat):
            part = part + got_lat[m, z]
        totals.append(part)
    projection[...] = jnp.broadcast_to(totals[0][own : own + 1], projection.shape)
    gram[lon] = jnp.concatenate([t[0:own] for t in totals], axis=0)
    third = []
    for d in range(1, nlon):
        k = nlon + d - 2
        copy = remote(gram.at[lon], gram.at[lon], sum_send.at[k], sum_recv.at[k], at(d, 0))
        copy.start()
        third.append(copy)
    for copy in third + late:
        copy.wait()


def smooth(nlon, nlat, *args):
    members = args[0].shape[0]
    slots, blocks = args[5].shape
    vm = pl.BlockSpec(memory_space=pltpu.VMEM)
    sds = jax.ShapeDtypeStruct
    lanes = 6 * slots
    pair = 2 * members
    dma = pltpu.SemaphoreType.DMA
    return pl.pallas_call(
        functools.partial(smooth_kernel, nlon, nlat),
        out_shape=(
            sds((16, pair, 256), BF),
            sds((nlon, 2 * members // nlon, pair), F32),
            sds((8, pair), F32),
            sds((16, 256), F32),
            sds((16, 256), F32),
            sds((2, 16, pair, 256), BF),
            sds((2, 16, 256), F32),
        ),
        in_specs=[pl.BlockSpec(memory_space=pltpu.MemorySpace.HBM)] * len(args),
        out_specs=(vm,) * 7,
        scratch_shapes=[
            pltpu.VMEM((members, 16, 256), BF),
            pltpu.VMEM((4, 16, 256), F32),
            pltpu.VMEM((16, 256), jnp.int32),
            pltpu.VMEM((slots, blocks), F32),
            pltpu.VMEM((slots, blocks), F32),
            pltpu.VMEM((slots, blocks), jnp.int32),
            pltpu.VMEM((1, blocks), jnp.int32),
            pltpu.VMEM((1, blocks), jnp.int32),
            pltpu.VMEM((2, members, 16, 256), BF),
            pltpu.VMEM((members // 16, 8, 8, 256), BF),
            pltpu.VMEM((members // 16, 8, 8, 256), BF),
            pltpu.VMEM((members // 16, 16, 128), BF),
            pltpu.VMEM((members // 16, 8, 128), BF),
            pltpu.VMEM((16, 128), F32),
            pltpu.VMEM((8, 128), F32),
            pltpu.VMEM((2, 8, 256), F32),
            pltpu.VMEM((2, 8, 256), F32),
            pltpu.VMEM((members // 16, 8, 8, 256), BF),
            pltpu.VMEM((members // 16, 8, 8, 256), BF),
            pltpu.VMEM((2, members // 16, 16, 128), BF),
            pltpu.VMEM((4, members // 16, 8, 128), BF),
            pltpu.VMEM((2, 8, 256), F32),
            pltpu.VMEM((2, 8, 256), F32),
            pltpu.VMEM((2, 16, 128), F32),
            pltpu.VMEM((4, 8, 128), F32),
            pltpu.VMEM((nlon, nlat, lanes), BF),
            pltpu.VMEM((nlon, nlat, lanes), BF),
            pltpu.VMEM((nlat, nlon, lanes), BF),
            pltpu.VMEM((nlat, nlon, lanes), BF),
            pltpu.VMEM((2, members * 32, 128), F32),
            pltpu.VMEM((5, 24, 384), F32),
            pltpu.VMEM((members // 16, 24, 128), F32),
            pltpu.VMEM((6, blocks // 2, 128), F32),
            pltpu.VMEM((32, 256), F32),
            pltpu.VMEM((32, 256), F32),
            pltpu.VMEM((16, members + 16, 256), BF),
            pltpu.VMEM((nlon, members // nlon + 1, pair), F32),
            pltpu.VMEM((2, nlat, members // nlon + 1, pair), F32),
            pltpu.VMEM((members // nlon + 1, pair), F32),
            pltpu.VMEM((nlon, members // nlon + 1, pair), F32),
            dma((12,)),
            dma((14,)),
            dma((14,)),
            dma((8,)),
            dma((8,)),
            dma((nlat - 1,)),
            dma((nlat - 1,)),
            dma((nlon - 1,)),
            dma((nlon - 1,)),
            dma((7,)),
            dma((7,)),
            dma((2 * nlon - 2,)),
            dma((2 * nlon - 2,)),
            dma((2 * nlat - 1,)),
            dma((2 * nlat - 1,)),
        ],
        compiler_params=pltpu.CompilerParams(
            collective_id=0, has_side_effects=True, vmem_limit_bytes=LIMIT
        ),
        name="smooth",
    )(*[pltpu.with_memory_space_constraint(a, pltpu.MemorySpace.HBM) for a in args])


def product(a, b):
    a_hi, b_hi = a.astype(BF), b.astype(BF)
    a_lo = (a - a_hi.astype(F32)).astype(BF)
    b_lo = (b - b_hi.astype(F32)).astype(BF)
    lhs = jnp.concatenate([a_hi, a_hi, a_lo], axis=1)
    rhs = jnp.concatenate([b_hi, b_lo, b_hi], axis=0)
    return jnp.dot(lhs, rhs, preferred_element_type=F32)


def inverse_root(gram, projection):
    n = gram.shape[0]
    identity = (iota((n, n), 0) == iota((n, n), 1)).astype(F32)
    system = (n - 1.0) * identity + 0.5 * (gram + gram.T)
    sums = jnp.sum(jnp.abs(system), axis=1, keepdims=True)
    bound = jnp.max(sums, axis=0, keepdims=True)
    iterate = system / bound
    factor = 1.5 * identity - 0.5 * iterate
    iterate = product(iterate, factor)
    accum = factor
    for _ in range(NS_ITERS - 2):
        factor = 1.5 * identity - 0.5 * product(accum, iterate)
        both = product(jnp.concatenate([iterate, accum], axis=0), factor)
        iterate, accum = both[0:n], both[n:]
    factor = 1.5 * identity - 0.5 * product(accum, iterate)
    root = product(factor, accum) / jnp.sqrt(bound)
    inner = jnp.sum(root * projection, axis=1, keepdims=True)
    weights = jnp.sum(root * inner, axis=0, keepdims=True)
    return root, weights


def analysis_kernel(
    gram,
    projection,
    now,
    lag,
    ocean,
    mean,
    lag_means,
    out,
    mean_out,
    transform,
    left,
    stage,
):
    step = pl.program_id(0)
    mem = lax.axis_index("mem")
    members = now.shape[1]
    own = members // 2
    base = pl.multiple_of(mem * own, own)

    @pl.when(step == 0)
    def _():
        n = members
        few = gram.shape[1] // 2
        for x in range(gram.shape[0]):
            for m in range(2):
                start = m * own + few * x
                transform[start : start + few] = gram[x, few * m : few * m + few]
        root, weights = inverse_root(transform[...], projection[0:1])
        transform[...] = jnp.sqrt(n - 1.0) * root
        left[0:own] = transform[pl.ds(base, own), :].astype(BF)
        left[own : own + 16] = jnp.broadcast_to(weights, (16, n)).astype(BF)

    wet = ocean[...]

    def update(x, own_x, r, mean_row):
        moved = jnp.dot(left[...], x, preferred_element_type=F32)
        s = own_x.astype(F32)
        w = wet[r : r + 1]
        blended = s + w * (moved[0:own] - s)
        for h in range(2):
            rows = pl.ds(h * own * 16 + r, own, stride=16)
            stage[rows, :] = blended[:, 128 * h : 128 * h + 128]
        mean_out[0, r : r + 1] = mean_row + w * moved[own : own + 1]

    @pl.when(step == 0)
    def _():
        for r in range(16):
            update(now[r], now[r, pl.ds(base, own), :], r, mean[r : r + 1])

    @pl.when(step > 0)
    def _():
        for r in range(16):
            update(lag[0, r], lag[0, r, pl.ds(base, own), :], r, lag_means[0, r : r + 1])

    for h in range(2):
        part = stage[h * own * 16 : (h + 1) * own * 16]
        out[0, :, :, 128 * h : 128 * h + 128] = part.reshape(own, 16, 128).astype(BF)


def analysis(gram, projection, now, lag, ocean, mean, lag_means):
    members = now.shape[1]
    own = members // 2
    vm = pl.BlockSpec(memory_space=pltpu.VMEM)
    sds = jax.ShapeDtypeStruct

    def lagged(s):
        return jnp.maximum(s - 1, 0)

    lag_spec = pl.BlockSpec((1, 16, members, 256), lambda s: (lagged(s), 0, 0, 0))
    return pl.pallas_call(
        analysis_kernel,
        grid=(3,),
        out_shape=(sds((3, own, 16, 256), BF), sds((3, 16, 256), F32)),
        in_specs=[vm, vm, vm, lag_spec, vm, vm]
        + [pl.BlockSpec((1, 16, 256), lambda s: (lagged(s), 0, 0))],
        out_specs=(
            pl.BlockSpec((1, own, 16, 256), lambda s: (s, 0, 0, 0)),
            pl.BlockSpec((1, 16, 256), lambda s: (s, 0, 0)),
        ),
        scratch_shapes=[
            pltpu.VMEM((members, members), F32),
            pltpu.VMEM((own + 16, members), BF),
            pltpu.VMEM((own * 32, 128), F32),
        ],
        compiler_params=pltpu.CompilerParams(vmem_limit_bytes=LIMIT),
        name="analysis",
    )(gram, projection, now, lag, ocean, mean, lag_means)


def body(
    nlon,
    nlat,
    anomalies,
    state_mean,
    delayed_deviation_pair,
    lagged_means,
    courant_lon,
    courant_lat,
    ocean,
    obs_values,
    obs_variance,
    obs_cells,
    obs_tile,
    obs_count,
):
    now, gram, projection, prior_mean, wet, lag, lag_means = smooth(
        nlon,
        nlat,
        anomalies,
        state_mean,
        courant_lon,
        courant_lat,
        ocean,
        obs_values.T,
        obs_variance.T,
        obs_cells.T,
        obs_tile.reshape(1, -1),
        obs_count.reshape(1, -1),
        delayed_deviation_pair,
        lagged_means,
    )
    return analysis(gram, projection, now, lag, wet, prior_mean, lag_means)


def solution(mesh):
    return jax.shard_map(
        functools.partial(body, mesh.shape["lon"], mesh.shape["lat"]),
        mesh=mesh,
        in_specs=(
            P("mem", "lat", "lon"),
            P("lat", "lon"),
            P(None, "mem", "lat", "lon"),
            P(None, "lat", "lon"),
            P("lat", "lon"),
            P("lat", "lon"),
            P("lat", "lon"),
            P(LON_LAT, None),
            P(LON_LAT, None),
            P(LON_LAT, None),
            P(LON_LAT, None),
            P(LON_LAT),
        ),
        out_specs=(P(None, "mem", "lat", "lon"), P(None, "lat", "lon")),
        check_vma=False,
    )
```

```python
import functools

import jax
import jax.numpy as jnp
from jax import lax
from jax.experimental import pallas as pl
from jax.experimental.pallas import tpu as pltpu
from jax.sharding import PartitionSpec as P

SUBSTEPS = 4
NS_ITERS = 8
BF = jnp.bfloat16
F32 = jnp.float32
MESH_ID = pl.DeviceIdType.MESH
LIMIT = 48 * 1024 * 1024
NT = (((1,), (1,)), ((), ()))

LON_LAT = ("lon", "lat")
SIDES = ((1, 0), (-1, 0), (1, 1), (1, -1), (-1, 1), (-1, -1))


def iota(shape, dim):
    return lax.broadcasted_iota(jnp.int32, shape, dim)


def remote(src, dst, send, recv, where):
    return pltpu.make_async_remote_copy(
        src_ref=src,
        dst_ref=dst,
        send_sem=send,
        recv_sem=recv,
        device_id=where,
        device_id_type=MESH_ID,
    )


def spot(lon, lat, mem):
    return {"lon": lon, "lat": lat, "mem": mem}


def row_of_all(stage, r, members):
    half = members * 16
    parts = [stage[pl.ds(h * half + r, members, stride=16), :] for h in range(2)]
    return jnp.concatenate(parts, axis=1)


def greet(places):
    barrier = pltpu.get_barrier_semaphore()
    for place in places:
        pl.semaphore_signal(barrier, inc=1, device_id=place, device_id_type=MESH_ID)
    return barrier, len(places)


def smooth_kernel(
    nlon,
    nlat,
    anom_in,
    mean_in,
    cx_in,
    cy_in,
    ocean_in,
    values_in,
    variance_in,
    cells_in,
    tile_in,
    count_in,
    lagged_in,
    lag_means_in,
    everyone,
    gram,
    projection,
    mean_out,
    wet_out,
    lag_all,
    lag_means,
    anom,
    fields,
    ocean,
    values,
    variance,
    cells,
    tile,
    count,
    lag_near,
    to_south,
    to_north,
    edges,
    corners,
    field_edges,
    field_corner,
    field_south_out,
    field_north_out,
    from_north,
    from_south,
    beside,
    beyond,
    field_north,
    field_south,
    field_beside,
    field_beyond,
    placed,
    midway,
    turned,
    arrived,
    stage,
    coef,
    side,
    planes,
    cell,
    cell_other,
    left,
    parts,
    got_lat,
    mine,
    got_lon,
    load_sem,
    halo_send,
    halo_recv,
    chunk_send,
    chunk_recv,
    lat_send,
    lat_recv,
    lon_send,
    lon_recv,
    pair_send,
    pair_recv,
    sum_send,
    sum_recv,
    all_send,
    all_recv,
):
    lon, lat, mem = lax.axis_index("lon"), lax.axis_index("lat"), lax.axis_index("mem")
    twin = spot(lon, lat, 1 - mem)
    members = anom.shape[0]
    base = pl.multiple_of(mem * members, members)

    def at(dx, dy, m=mem):
        return spot(lax.rem(lon + dx + nlon, nlon), lax.rem(lat + dy + nlat, nlat), m)

    loads = [
        pltpu.make_async_copy(src, dst, load_sem.at[i])
        for i, (src, dst) in enumerate(
            (
                (anom_in, anom),
                (mean_in, fields.at[0]),
                (cx_in, fields.at[1]),
                (cy_in, fields.at[2]),
                (ocean_in, ocean),
                (tile_in, tile),
                (count_in, count),
                (values_in, values),
                (variance_in, variance),
                (cells_in, cells),
                (lagged_in, lag_near),
                (lag_means_in, lag_means),
            )
        )
    ]
    for load in loads[:5]:
        load.start()
    across = [(d, m) for m in (0, 1) for d in range(nlat) if d or m]

    def other(m):
        return mem + m - 2 * mem * m

    peers = [at(0, d, other(m)) for d, m in across]
    peers += [at(d, 0) for d in range(1, nlon)]
    peers += [at(dx, dy) for dx, dy in SIDES if dy != 0]
    barrier, total = greet(peers)
    for load in loads[5:]:
        load.start()

    for load in loads[:5]:
        load.wait()
    fields[3] = ocean[...].astype(F32)
    wet_out[...] = fields[3]
    chunks = members // 16

    def banded(x, above):
        low, high = x[:, : x.shape[1] // 2], x[:, x.shape[1] // 2 :]
        if above:
            low = pltpu.roll(low, 4, 2)
        else:
            high = pltpu.roll(high, 4, 2)
        return jnp.where(iota(low.shape, 2) < 4, low, high)

    top = anom[:, 0:8, :].astype(F32).reshape(chunks, 16, 8, 256)
    to_south[...] = banded(top, False).astype(BF)
    bottom = anom[:, 8:16, :].astype(F32).reshape(chunks, 16, 8, 256)
    to_north[...] = banded(bottom, True).astype(BF)
    field_south_out[...] = banded(fields[:, 0:8, :].reshape(1, 4, 8, 256), False)[0]
    field_north_out[...] = banded(fields[:, 8:16, :].reshape(1, 4, 8, 256), True)[0]
    lane16 = iota((16, 128), 1)

    def both_edges(x):
        return jnp.where(lane16 < 64, x[:, 0:128], x[:, 128:256])

    def packed(member, number):
        out = jnp.zeros((16, 128), F32)
        for k in range(number):
            moved = pltpu.roll(both_edges(member(k)), 8 * k, 1) if k else both_edges(member(k))
            owner = ((lane16 + 4) % 128) // 8 == k
            out = jnp.where(owner, moved, out)
        return out

    sub8, lane8 = iota((8, 128), 0), iota((8, 128), 1)

    def corner(x):
        return jnp.where(sub8 < 4, x[0:8], x[8:16])

    packed_fields = packed(lambda k: fields[k], 4)
    field_edges[...] = packed_fields
    field_corner[...] = corner(packed_fields)
    for g in range(chunks):
        packed_group = packed(lambda k: anom[16 * g + k].astype(F32), 16)
        edges[g] = packed_group.astype(BF)
        corners[g] = corner(packed_group).astype(BF)

    pl.semaphore_wait(barrier, total)

    first = []
    for d in range(1, nlon):
        to = lax.rem(lon + d, nlon)
        k = d - 1
        first.append(
            remote(placed.at[to], midway.at[lon], lon_send.at[k], lon_recv.at[k], at(d, 0))
        )
    halo = []
    pieces = [(field_south_out, field_north, 0, -1), (field_north_out, field_south, 0, 1)]
    for i, (dx, dy) in enumerate(SIDES[:2]):
        pieces.append((edges, beside.at[i], -dx, -dy))
        pieces.append((field_edges, field_beside.at[i], -dx, -dy))
    for i, (dx, dy) in enumerate(SIDES[2:]):
        pieces.append((corners, beyond.at[i], -dx, -dy))
        pieces.append((field_corner, field_beyond.at[i], -dx, -dy))
    for i, (src, dst, dx, dy) in enumerate(pieces):
        halo.append(remote(src, dst, halo_send.at[i], halo_recv.at[i], at(dx, dy)))
    bands = []
    for c in range(chunks):
        for j, (src, dst, dy) in enumerate(
            ((to_south, from_north, -1), (to_north, from_south, 1))
        ):
            k = 2 * c + j
            bands.append(
                remote(src.at[c], dst.at[c], chunk_send.at[k], chunk_recv.at[k], at(0, dy))
            )
    for copy in halo + bands:
        copy.start()
    for load in loads[5:10]:
        load.wait()
    slots, blocks = values.shape
    row_i, col_i = iota((blocks, blocks), 0), iota((blocks, blocks), 1)
    tile_row = jnp.broadcast_to(tile[...].astype(F32), (blocks, blocks))
    tile_col = jnp.sum(jnp.where(row_i == col_i, tile_row, 0.0), axis=1, keepdims=True)
    before = (tile_col == tile_row) & (row_i < col_i)
    rank = jnp.sum(jnp.where(before, 1.0, 0.0), axis=0, keepdims=True)
    chosen = (row_i.astype(F32) == tile_row) & (rank == mem.astype(F32))
    selection = jnp.where(chosen, 1.0, 0.0).astype(BF)
    valid = iota((slots, blocks), 0) < count[...]
    weight = jnp.where(valid, 1.0 / variance[...], 0.0)
    scaled = weight * values[...]
    where = cells[...]
    w_hi = weight.astype(BF).astype(F32)
    v_hi = scaled.astype(BF).astype(F32)
    payload = jnp.concatenate(
        [
            w_hi,
            weight - w_hi,
            v_hi,
            scaled - v_hi,
            (where // 256).astype(F32),
            (where % 256).astype(F32),
        ],
        axis=0,
    ).astype(BF)
    spread = lax.dot_general(selection, payload, NT, preferred_element_type=F32)
    placed[...] = spread.reshape(nlon, nlat, 6 * slots).astype(BF)

    for copy in first:
        copy.start()
    midway[lon] = placed[lon]

    loads[10].wait()
    loads[11].wait()
    late = []
    for which in range(2):
        for h in range(2):
            part = lag_near[which, :, :, 128 * h : 128 * h + 128].astype(F32)
            stage[which, h * members * 16 : (h + 1) * members * 16] = part.reshape(-1, 128)
        for r in range(16):
            row = row_of_all(stage.at[which], r, members)
            lag_all[which, r, pl.ds(base, members), :] = row.astype(BF)
        ours = lag_all.at[which, :, pl.ds(base, members), :]
        late.append(remote(ours, ours, pair_send.at[5 + which], pair_recv.at[5 + which], twin))
        late[-1].start()

    for copy in first:
        copy.wait()
    swap = (row_i // nlon == col_i % nlat) & (row_i % nlon == col_i // nlat)
    mixed = midway[...].astype(F32).reshape(blocks, 6 * slots).astype(BF)
    ordered = jnp.dot(jnp.where(swap, 1.0, 0.0).astype(BF), mixed, preferred_element_type=F32)
    turned[...] = ordered.reshape(nlat, nlon, 6 * slots).astype(BF)
    second = []
    for d in range(1, nlat):
        to = lax.rem(lat + d, nlat)
        copy = remote(
            turned.at[to], arrived.at[lat], lat_send.at[d - 1], lat_recv.at[d - 1], at(0, d)
        )
        copy.start()
        second.append(copy)
    arrived[lat] = turned[lat]
    for copy in halo:
        copy.wait()
    north_ok = lat < nlat - 1
    south_ok = lat > 0

    def sides(east, west, north_east, south_east, north_west, south_west):
        core = jnp.where(lane16 % 8 < 4, east, west)
        is_east = lane8 % 8 < 4
        up = jnp.where(is_east, north_east, north_west)
        down = jnp.where(is_east, south_east, south_west)
        up = jnp.where(north_ok, up, 0.0)
        down = jnp.where(south_ok, down, 0.0)
        return jnp.concatenate([core, jnp.where(sub8 < 4, up, down)], axis=0)

    for g in range(chunks):
        near = [beside[i, g].astype(F32) for i in range(2)]
        side[g] = sides(*near, *[beyond[i, g].astype(F32) for i in range(4)])
    field_side = sides(*[field_beside[i] for i in range(2)], *[field_beyond[i] for i in range(4)])
    lane24 = iota((24, 128), 1)
    keep = (lane24 < 4) | (lane24 >= 124)
    subw = iota((8, 256), 0)

    def whole(core, up, down, turned):
        outer = jnp.where(subw < 4, jnp.where(north_ok, up, 0.0), jnp.where(south_ok, down, 0.0))
        return jnp.concatenate([jnp.concatenate([core, outer], axis=0), turned], axis=1)

    extended = []
    for k in range(4):
        turn = pltpu.roll(field_side, 128 - 8 * k, 1) if k else field_side
        turn = jnp.where(keep, turn, 0.0)
        up, down = field_north[k % 2], field_south[k % 2]
        if k < 2:
            down = pltpu.roll(down, 4, 0)
        else:
            up = pltpu.roll(up, 4, 0)
        extended.append(whole(fields[k], up, down, turn))
    ex_mean, ex_x, ex_y, ex_wet = extended
    coef[0] = ex_wet * jnp.maximum(ex_x, 0.0)
    coef[1] = -ex_wet * jnp.minimum(ex_x, 0.0)
    coef[2] = ex_wet * jnp.maximum(ex_y, 0.0)
    coef[3] = -ex_wet * jnp.minimum(ex_y, 0.0)
    coef[4] = 1.0 - ((coef[0] + coef[1]) + (coef[2] + coef[3]))

    def substep(group):
        tiles = [
            [[q[8 * r : 8 * r + 8, 128 * c : 128 * c + 128] for c in range(3)] for r in range(3)]
            for q in group
        ]
        new = [[[None] * 3 for _ in range(3)] for _ in group]
        for r in range(3):
            for c in range(3):
                a, b, d, e, keep_own = [
                    coef[k, 8 * r : 8 * r + 8, 128 * c : 128 * c + 128] for k in range(5)
                ]
                for t, out in zip(tiles, new):
                    q = t[r][c]
                    west = pltpu.roll(jnp.where(lane8 == 127, t[r][c - 1], q), 1, 1)
                    east = pltpu.roll(jnp.where(lane8 == 0, t[r][(c + 1) % 3], q), 127, 1)
                    south = pltpu.roll(jnp.where(sub8 == 7, t[r - 1][c], q), 1, 0)
                    north = pltpu.roll(jnp.where(sub8 == 0, t[(r + 1) % 3][c], q), 7, 0)
                    out[r][c] = (keep_own * q + a * west) + (b * east + d * south) + e * north
        return [
            jnp.concatenate([jnp.concatenate(row, axis=1) for row in out], axis=0) for out in new
        ]

    swaps = []

    def advance(c):
        for copy in bands[2 * c : 2 * c + 2]:
            copy.wait()
        where_to, group = [], []
        for i in range(8):
            north, south = from_north[c, i].astype(F32), from_south[c, i].astype(F32)
            for later in (0, 8):
                m = 16 * c + i + later
                up = pltpu.roll(north, 4, 0) if later else north
                down = south if later else pltpu.roll(south, 4, 0)
                turn = (128 - 8 * (i + later)) % 128
                turned_side = pltpu.roll(side[c], turn, 1) if turn else side[c]
                where_to.append(m)
                group.append(whole(anom[m].astype(F32), up, down, turned_side))
        if c == 0:
            group.append(ex_mean)
        for _ in range(SUBSTEPS):
            group = sum([substep(group[k : k + 4]) for k in range(0, len(group), 4)], [])
        if c == 0:
            mean_out[...] = group.pop()[0:16, 0:256]
        for m, q in zip(where_to, group):
            for h in range(2):
                start = (h * members + m) * 16
                stage[0, start : start + 16, :] = q[0:16, 128 * h : 128 * h + 128]
        rows = pl.ds(pl.multiple_of(base + 16 * c, 16), 16)
        for r in range(16):
            parts_of_row = [
                stage[0, pl.ds((h * members + 16 * c) * 16 + r, 16, stride=16), :]
                for h in range(2)
            ]
            everyone[r, rows, :] = jnp.concatenate(parts_of_row, axis=1).astype(BF)
        ours = everyone.at[:, rows, :]
        swaps.append(remote(ours, ours, pair_send.at[c], pair_recv.at[c], twin))
        swaps[-1].start()

    advance(0)
    for c in range(1, chunks - 1):
        advance(c)

    advance(chunks - 1)

    for copy in second:
        copy.wait()
    table = arrived[...].astype(F32).reshape(blocks, 6 * slots)
    pairs = blocks // 2
    near = iota((pairs, 128), 1) < 64
    for j in range(3):
        a = table[0:pairs, 128 * j : 128 * (j + 1)]
        b = table[pairs:blocks, 128 * j : 128 * (j + 1)]
        planes[2 * j] = jnp.where(near, a, pltpu.roll(b, 64, 1))
        planes[2 * j + 1] = jnp.where(near, pltpu.roll(a, 64, 1), b)
    row_id = iota((16, 256), 0).astype(F32)
    col_id = iota((256, 256), 0).astype(F32)

    def histogram(s, acc):
        def two(p):
            return jnp.concatenate(
                [planes[p, pl.ds(2 * s, 1), :], planes[p, pl.ds(2 * s + 1, 1), :]], axis=1
            )

        hit = row_id == two(4)
        lhs = jnp.concatenate([jnp.where(hit, two(p), 0.0) for p in range(4)], axis=0)
        rhs = jnp.where(col_id == two(5), 1.0, 0.0)
        return acc + lax.dot_general(lhs.astype(BF), rhs.astype(BF), NT, preferred_element_type=F32)

    acc = lax.fori_loop(0, pairs // 2, histogram, jnp.zeros((64, 256), F32), unroll=16)
    cell[0:16] = acc[0:16] + acc[16:32]
    cell[16:32] = acc[32:48] + acc[48:64]
    swap_cells = remote(cell, cell_other, pair_send.at[4], pair_recv.at[4], twin)
    swap_cells.start()


    swap_cells.wait()
    sums = cell[...] + cell_other[...]
    weight = sums[0:16]
    misfit = sums[16:32] - weight * mean_out[...]
    for r in range(16):
        x = everyone[r, pl.ds(base, members), :].astype(F32)
        left[r, 0:members] = (x * weight[r : r + 1]).astype(BF)
        left[r, members : members + 16] = jnp.broadcast_to(misfit[r : r + 1], (16, 256)).astype(BF)
    acc = jnp.zeros((members + 16, 2 * members), F32)
    for copy in swaps:
        copy.wait()
    for r in range(16):
        acc = acc + lax.dot_general(left[r], everyone[r], NT, preferred_element_type=F32)
    own = members // nlon
    for x in range(nlon):
        parts[x, 0:own] = acc[own * x : own * x + own]
        parts[x, own : own + 1] = acc[members : members + 1]

    first = []
    for d in range(1, nlon):
        to = lax.rem(lon + d, nlon)
        k = d - 1
        copy = remote(parts.at[to], got_lon.at[lon], sum_send.at[k], sum_recv.at[k], at(d, 0))
        copy.start()
        first.append(copy)
    got_lon[lon] = parts[lon]
    for copy in first:
        copy.wait()
    part = got_lon[0]
    for x in range(1, nlon):
        part = part + got_lon[x]
    mine[...] = part

    second = []
    for i, (d, m) in enumerate(across):
        copy = remote(
            mine, got_lat.at[mem, lat], all_send.at[i], all_recv.at[i], at(0, d, other(m))
        )
        copy.start()
        second.append(copy)
    got_lat[mem, lat] = part
    for copy in second:
        copy.wait()
    totals = []
    for m in range(2):
        part = got_lat[m, 0]
        for z in range(1, nlat):
            part = part + got_lat[m, z]
        totals.append(part)
    projection[...] = jnp.broadcast_to(totals[0][own : own + 1], projection.shape)
    gram[lon] = jnp.concatenate([t[0:own] for t in totals], axis=0)
    third = []
    for d in range(1, nlon):
        k = nlon + d - 2
        copy = remote(gram.at[lon], gram.at[lon], sum_send.at[k], sum_recv.at[k], at(d, 0))
        copy.start()
        third.append(copy)
    for copy in third + late:
        copy.wait()


def smooth(nlon, nlat, *args):
    members = args[0].shape[0]
    slots, blocks = args[5].shape
    vm = pl.BlockSpec(memory_space=pltpu.VMEM)
    sds = jax.ShapeDtypeStruct
    lanes = 6 * slots
    pair = 2 * members
    dma = pltpu.SemaphoreType.DMA
    return pl.pallas_call(
        functools.partial(smooth_kernel, nlon, nlat),
        out_shape=(
            sds((16, pair, 256), BF),
            sds((nlon, 2 * members // nlon, pair), F32),
            sds((8, pair), F32),
            sds((16, 256), F32),
            sds((16, 256), F32),
            sds((2, 16, pair, 256), BF),
            sds((2, 16, 256), F32),
        ),
        in_specs=[pl.BlockSpec(memory_space=pltpu.MemorySpace.HBM)] * len(args),
        out_specs=(vm,) * 7,
        scratch_shapes=[
            pltpu.VMEM((members, 16, 256), BF),
            pltpu.VMEM((4, 16, 256), F32),
            pltpu.VMEM((16, 256), jnp.int32),
            pltpu.VMEM((slots, blocks), F32),
            pltpu.VMEM((slots, blocks), F32),
            pltpu.VMEM((slots, blocks), jnp.int32),
            pltpu.VMEM((1, blocks), jnp.int32),
            pltpu.VMEM((1, blocks), jnp.int32),
            pltpu.VMEM((2, members, 16, 256), BF),
            pltpu.VMEM((members // 16, 8, 8, 256), BF),
            pltpu.VMEM((members // 16, 8, 8, 256), BF),
            pltpu.VMEM((members // 16, 16, 128), BF),
            pltpu.VMEM((members // 16, 8, 128), BF),
            pltpu.VMEM((16, 128), F32),
            pltpu.VMEM((8, 128), F32),
            pltpu.VMEM((2, 8, 256), F32),
            pltpu.VMEM((2, 8, 256), F32),
            pltpu.VMEM((members // 16, 8, 8, 256), BF),
            pltpu.VMEM((members // 16, 8, 8, 256), BF),
            pltpu.VMEM((2, members // 16, 16, 128), BF),
            pltpu.VMEM((4, members // 16, 8, 128), BF),
            pltpu.VMEM((2, 8, 256), F32),
            pltpu.VMEM((2, 8, 256), F32),
            pltpu.VMEM((2, 16, 128), F32),
            pltpu.VMEM((4, 8, 128), F32),
            pltpu.VMEM((nlon, nlat, lanes), BF),
            pltpu.VMEM((nlon, nlat, lanes), BF),
            pltpu.VMEM((nlat, nlon, lanes), BF),
            pltpu.VMEM((nlat, nlon, lanes), BF),
            pltpu.VMEM((2, members * 32, 128), F32),
            pltpu.VMEM((5, 24, 384), F32),
            pltpu.VMEM((members // 16, 24, 128), F32),
            pltpu.VMEM((6, blocks // 2, 128), F32),
            pltpu.VMEM((32, 256), F32),
            pltpu.VMEM((32, 256), F32),
            pltpu.VMEM((16, members + 16, 256), BF),
            pltpu.VMEM((nlon, members // nlon + 1, pair), F32),
            pltpu.VMEM((2, nlat, members // nlon + 1, pair), F32),
            pltpu.VMEM((members // nlon + 1, pair), F32),
            pltpu.VMEM((nlon, members // nlon + 1, pair), F32),
            dma((12,)),
            dma((14,)),
            dma((14,)),
            dma((8,)),
            dma((8,)),
            dma((nlat - 1,)),
            dma((nlat - 1,)),
            dma((nlon - 1,)),
            dma((nlon - 1,)),
            dma((7,)),
            dma((7,)),
            dma((2 * nlon - 2,)),
            dma((2 * nlon - 2,)),
            dma((2 * nlat - 1,)),
            dma((2 * nlat - 1,)),
        ],
        compiler_params=pltpu.CompilerParams(
            collective_id=0, has_side_effects=True, vmem_limit_bytes=LIMIT
        ),
        name="smooth",
    )(*[pltpu.with_memory_space_constraint(a, pltpu.MemorySpace.HBM) for a in args])


def product(a, b):
    a_hi, b_hi = a.astype(BF), b.astype(BF)
    a_lo = (a - a_hi.astype(F32)).astype(BF)
    b_lo = (b - b_hi.astype(F32)).astype(BF)
    lhs = jnp.concatenate([a_hi, a_hi, a_lo], axis=1)
    rhs = jnp.concatenate([b_hi, b_lo, b_hi], axis=0)
    return jnp.dot(lhs, rhs, preferred_element_type=F32)


def inverse_root(gram, projection):
    n = gram.shape[0]
    identity = (iota((n, n), 0) == iota((n, n), 1)).astype(F32)
    system = (n - 1.0) * identity + 0.5 * (gram + gram.T)
    sums = jnp.sum(jnp.abs(system), axis=1, keepdims=True)
    bound = jnp.max(sums, axis=0, keepdims=True)
    iterate = system / bound
    factor = 1.5 * identity - 0.5 * iterate
    iterate = product(iterate, factor)
    accum = factor
    for _ in range(NS_ITERS - 2):
        factor = 1.5 * identity - 0.5 * product(accum, iterate)
        both = product(jnp.concatenate([iterate, accum], axis=0), factor)
        iterate, accum = both[0:n], both[n:]
    factor = 1.5 * identity - 0.5 * product(accum, iterate)
    root = product(factor, accum) / jnp.sqrt(bound)
    inner = jnp.sum(root * projection, axis=1, keepdims=True)
    weights = jnp.sum(root * inner, axis=0, keepdims=True)
    return root, weights


def analysis_kernel(
    gram,
    projection,
    now,
    lag,
    ocean,
    mean,
    lag_means,
    out,
    mean_out,
    transform,
    left,
    stage,
):
    step = pl.program_id(0)
    mem = lax.axis_index("mem")
    members = now.shape[1]
    own = members // 2
    base = pl.multiple_of(mem * own, own)

    @pl.when(step == 0)
    def _():
        n = members
        few = gram.shape[1] // 2
        for x in range(gram.shape[0]):
            for m in range(2):
                start = m * own + few * x
                transform[start : start + few] = gram[x, few * m : few * m + few]
        root, weights = inverse_root(transform[...], projection[0:1])
        transform[...] = jnp.sqrt(n - 1.0) * root
        left[0:own] = transform[pl.ds(base, own), :].astype(BF)
        left[own : own + 16] = jnp.broadcast_to(weights, (16, n)).astype(BF)

    wet = ocean[...]

    def update(x, own_x, r, mean_row):
        moved = jnp.dot(left[...], x, preferred_element_type=F32)
        s = own_x.astype(F32)
        w = wet[r : r + 1]
        blended = s + w * (moved[0:own] - s)
        for h in range(2):
            rows = pl.ds(h * own * 16 + r, own, stride=16)
            stage[rows, :] = blended[:, 128 * h : 128 * h + 128]
        mean_out[0, r : r + 1] = mean_row + w * moved[own : own + 1]

    @pl.when(step == 0)
    def _():
        for r in range(16):
            update(now[r], now[r, pl.ds(base, own), :], r, mean[r : r + 1])

    @pl.when(step > 0)
    def _():
        for r in range(16):
            update(lag[0, r], lag[0, r, pl.ds(base, own), :], r, lag_means[0, r : r + 1])

    for h in range(2):
        part = stage[h * own * 16 : (h + 1) * own * 16]
        out[0, :, :, 128 * h : 128 * h + 128] = part.reshape(own, 16, 128).astype(BF)


def analysis(gram, projection, now, lag, ocean, mean, lag_means):
    members = now.shape[1]
    own = members // 2
    vm = pl.BlockSpec(memory_space=pltpu.VMEM)
    sds = jax.ShapeDtypeStruct

    def lagged(s):
        return jnp.maximum(s - 1, 0)

    lag_spec = pl.BlockSpec((1, 16, members, 256), lambda s: (lagged(s), 0, 0, 0))
    return pl.pallas_call(
        analysis_kernel,
        grid=(3,),
        out_shape=(sds((3, own, 16, 256), BF), sds((3, 16, 256), F32)),
        in_specs=[vm, vm, vm, lag_spec, vm, vm]
        + [pl.BlockSpec((1, 16, 256), lambda s: (lagged(s), 0, 0))],
        out_specs=(
            pl.BlockSpec((1, own, 16, 256), lambda s: (s, 0, 0, 0)),
            pl.BlockSpec((1, 16, 256), lambda s: (s, 0, 0)),
        ),
        scratch_shapes=[
            pltpu.VMEM((members, members), F32),
            pltpu.VMEM((own + 16, members), BF),
            pltpu.VMEM((own * 32, 128), F32),
        ],
        compiler_params=pltpu.CompilerParams(vmem_limit_bytes=LIMIT),
        name="analysis",
    )(gram, projection, now, lag, ocean, mean, lag_means)


def body(
    nlon,
    nlat,
    anomalies,
    state_mean,
    delayed_deviation_pair,
    lagged_means,
    courant_lon,
    courant_lat,
    ocean,
    obs_values,
    obs_variance,
    obs_cells,
    obs_tile,
    obs_count,
):
    now, gram, projection, prior_mean, wet, lag, lag_means = smooth(
        nlon,
        nlat,
        anomalies,
        state_mean,
        courant_lon,
        courant_lat,
        ocean,
        obs_values.T,
        obs_variance.T,
        obs_cells.T,
        obs_tile.reshape(1, -1),
        obs_count.reshape(1, -1),
        delayed_deviation_pair,
        lagged_means,
    )
    return analysis(gram, projection, now, lag, wet, prior_mean, lag_means)


def solution(mesh):
    return jax.shard_map(
        functools.partial(body, mesh.shape["lon"], mesh.shape["lat"]),
        mesh=mesh,
        in_specs=(
            P("mem", "lat", "lon"),
            P("lat", "lon"),
            P(None, "mem", "lat", "lon"),
            P(None, "lat", "lon"),
            P("lat", "lon"),
            P("lat", "lon"),
            P("lat", "lon"),
            P(LON_LAT, None),
            P(LON_LAT, None),
            P(LON_LAT, None),
            P(LON_LAT, None),
            P(LON_LAT),
        ),
        out_specs=(P(None, "mem", "lat", "lon"), P(None, "lat", "lon")),
        check_vma=False,
    )
```
